32 devices in a mesh: grp: 16 (over z, y, core), sub: 2 (over x).
Axes of the slice: x: 2, y: 2, z: 4, core: 2. Of those that a mesh axis runs over, the one named last changes fastest.
Arguments:
- displacement: float32 [128, 32, 256], P('grp', 'sub'), may hold values from -2 to 2
- load: float32 [128, 32, 256], P('grp', 'sub'), may hold values from -6 to 6
- kl_coef: float32 [32], replicated, may hold values from -3 to 3
- damaged: int32 [16], replicated, may hold values from 0 to 1048575, as said below
- owner: int32 [16], replicated, may hold values from 0 to 15, each once
- phase: float32 [16, 32, 1024], P('grp', 'sub'), may hold values from 1 to 10
- soften: float32 [16, 32, 1024], P('grp', 'sub'), may hold values from 0.5 to 4
Outputs:
- step_field: float32 [128, 32, 256], P('grp', 'sub')
- residual: float32 [128, 32, 256], P('grp', 'sub')
- tangents: float32 [16, 9], replicated
- point_flux: float32 [16, 3], replicated
The draws below stay inside these ranges and needn't reach their ends.
Inputs may be any that keep to these rules, and one draw needn't show every extreme that they name: `damaged`: point p lies in rows p * 8 to (p + 1) * 8 - 1 of the first dimension, so the points are distinct cells. `owner`: each periodic cell resolves exactly one damaged point.
All inputs are finite; a program needn't handle non-finite values.
Results may differ from the reference program's by a relative error of at most 0.00045.
Values sent between devices are 32-bit elements; how exact they have to be, the bound alone decides.
A program may use at most 320 MiB of HBM per device.

```python
import math
import jax
import jax.numpy as jnp
from jax import lax

CX = 8
M = 32
MITERS = 4
CG_ITERS = 6
MODES = 32
NX = 128
NY = 32
NZ = 256
RVES = 16
DAMAGED = 16


def draw_damaged(key, part):
    key_x = jax.random.fold_in(key, 11)
    key_y = jax.random.fold_in(key, 12)
    key_z = jax.random.fold_in(key, 13)
    index = jnp.arange(DAMAGED, dtype=jnp.int32)
    rows_x = index * CX + jax.random.randint(key_x, (DAMAGED,), 0, CX, dtype=jnp.int32)
    rows_y = jax.random.randint(key_y, (DAMAGED,), 0, NY, dtype=jnp.int32)
    rows_z = jax.random.randint(key_z, (DAMAGED,), 0, NZ, dtype=jnp.int32)
    return ((rows_x * NY + rows_y) * NZ + rows_z).astype(jnp.int32)


def block_levels(own_key, dims, shards, low, largest):
    gain = 1.0
    for axis_at, blocks in shards:
        steps = jax.random.uniform(jax.random.fold_in(jax.random.fold_in(own_key, 6), axis_at), (blocks,), jnp.float32, low / len(shards), largest / len(shards))
        gain = gain * jnp.repeat(jnp.exp(steps), dims[axis_at] // blocks).reshape((-1,) + (1,) * (len(dims) - 1 - axis_at))
    return gain


def normal_values(own_key, shape, scale, reach, shards=(), kind=jnp.bfloat16):
    loudness = block_levels(own_key, shape, shards, -0.22, 0.18) if shards else 1.0
    result = jax.random.normal(own_key, shape, jnp.float32) * scale * loudness
    return jnp.minimum(jnp.maximum(result, -reach), reach).astype(kind)


def setup_inputs(seed: int = 0) -> dict:
    key_list = jax.random.split(jax.random.key(seed), 8)
    return {
        "displacement": normal_values(key_list[0], (NX, NY, NZ), 0.3, 2.0, ((0, 16), (1, 2)), jnp.float32),
        "load": normal_values(key_list[1], (NX, NY, NZ), 1.0, 6.0, ((0, 16), (1, 2)), jnp.float32),
        "kl_coef": normal_values(key_list[2], (MODES,), 1.0, 3.0, (), jnp.float32),
        "damaged": draw_damaged(jax.random.fold_in(key_list[7], 71), 0),
        "owner": jax.random.permutation(key_list[4], RVES).astype(jnp.int32),
        "phase": jnp.clip(jnp.exp(math.log(10.0) - 2.3025851 * jax.random.uniform(key_list[5], (RVES, M, M * M), jnp.float32) ** block_levels(key_list[5], (RVES, M, M * M), ((0, 16), (1, 2)), -0.2, 0.2)), 1.0, 10.0),
        "soften": jnp.clip(jnp.exp(math.log(4.0) - 2.0794415 * jax.random.uniform(key_list[6], (RVES, M, M * M), jnp.float32) ** block_levels(key_list[6], (RVES, M, M * M), ((0, 16), (1, 2)), -0.2, 0.2)), 0.5, 4.0),
    }


K0 = 6.0
SHIFT = 0.002
HIGH = lax.Precision.HIGHEST


def conductivity(kl_coef, xs, ys, zs, total_x, total_y, total_z):
    order = jnp.arange(4, dtype=jnp.float32)[:, None] + 1.0
    base_x = jnp.cos(jnp.pi * order * (xs.astype(jnp.float32)[None] + 0.5) / total_x)
    base_y = jnp.cos(jnp.pi * order * (ys.astype(jnp.float32)[None] + 0.5) / total_y)
    base_z = jnp.cos(jnp.pi * order[:2] * (zs.astype(jnp.float32)[None] + 0.5) / total_z)
    coef = kl_coef.reshape(2, 4, 4)
    field = jnp.einsum("cba,ai,bj,ck->ijk", coef, base_x, base_y, base_z, precision=HIGH)
    return jnp.exp(0.4 * field)


def gradient(field):
    padded = jnp.pad(field, ((0, 1), (0, 1), (0, 1)))
    return jnp.stack([padded[1:, :-1, :-1] - field, padded[:-1, 1:, :-1] - field, padded[:-1, :-1, 1:] - field])


def divergence(grads, field, kcell, damaged, tensors):
    flux = kcell[None] * grads
    picked = grads.reshape(3, -1)[:, damaged]
    newval = jnp.einsum("pij,jp->ip", tensors, picked, precision=HIGH)
    flux = flux.reshape(3, -1).at[:, damaged].set(newval).reshape(grads.shape)
    padded = jnp.pad(flux, ((0, 0), (1, 0), (1, 0), (1, 0)))
    out = padded[0, :-1, 1:, 1:] - flux[0] + padded[1, 1:, :-1, 1:] - flux[1] + padded[2, 1:, 1:, :-1] - flux[2]
    return out + SHIFT * field


def micro(args):
    phase, soften, strain = args
    cond = (phase / (1.0 + soften * jnp.sum(strain * strain))).reshape(M, M, M)
    freq = jnp.arange(M, dtype=jnp.int32)
    line = 4.0 * jnp.sin(jnp.pi * freq.astype(jnp.float32) / M) ** 2
    lam = line[:, None, None] + line[None, :, None] + line[None, None, :]
    anchor = ((freq[:, None, None] + freq[None, :, None] + freq[None, None, :]) == 0).astype(jnp.float32)
    inverse = (1.0 - anchor) / (K0 * (lam + anchor))
    units = jnp.eye(3, dtype=jnp.float32)

    def strains(phi):
        return [units[:, i][:, None, None, None] + jnp.roll(phi, -1, axis=i + 1) - phi for i in range(3)]

    phi = jnp.zeros((3, M, M, M), jnp.float32)
    for sweep in range(MITERS):
        parts = strains(phi)
        tau = [(cond - K0) * parts[i] for i in range(3)]
        div = tau[0] - jnp.roll(tau[0], 1, axis=1)
        div = div + tau[1] - jnp.roll(tau[1], 1, axis=2)
        div = div + tau[2] - jnp.roll(tau[2], 1, axis=3)
        spectrum = jnp.fft.fftn(div, axes=(1, 2, 3)) * inverse
        phi = jnp.real(jnp.fft.ifftn(spectrum, axes=(1, 2, 3)))
    parts = strains(phi)
    table = jnp.stack([jnp.mean(cond * parts[i], axis=(1, 2, 3)) for i in range(3)])
    return 0.5 * (table + table.T)


def reference(displacement, load, kl_coef, damaged, owner, phase, soften):
    nx, ny, nz = displacement.shape
    kcell = conductivity(kl_coef, jnp.arange(nx), jnp.arange(ny), jnp.arange(nz), nx, ny, nz)
    grads = gradient(displacement)
    strain = grads.reshape(3, -1)[:, damaged].T
    select = (owner[None, :] == jnp.arange(RVES, dtype=jnp.int32)[:, None]).astype(jnp.float32)
    rve_strain = jnp.sum(select[:, :, None] * strain[None], axis=1)
    tangents = lax.map(micro, (phase, soften, rve_strain))
    tensors = tangents[owner]

    def operate(field):
        return divergence(gradient(field), field, kcell, damaged, tensors)

    rhs = load - divergence(grads, displacement, kcell, damaged, tensors)
    step_field = jnp.zeros_like(rhs)
    residual = rhs
    direction = rhs
    norm_now = jnp.sum(residual * residual)
    for sweep in range(CG_ITERS):
        image = operate(direction)
        alpha = norm_now / jnp.sum(direction * image)
        step_field = step_field + alpha * direction
        residual = residual - alpha * image
        norm_next = jnp.sum(residual * residual)
        direction = residual + (norm_next / norm_now) * direction
        norm_now = norm_next
    step_grads = gradient(step_field).reshape(3, -1)[:, damaged].T
    point_flux = jnp.einsum("pij,pj->pi", tensors, step_grads, precision=HIGH)
    return step_field, residual, tangents.reshape(RVES, 9), point_flux
```

```python
import functools
import math

import jax
import jax.numpy as jnp
import numpy as np
from jax import lax
from jax.experimental import pallas as pl
from jax.experimental.pallas import tpu as pltpu
from jax.sharding import PartitionSpec as P

CG_ITERS = 6
BLOCK = CG_ITERS // 2
NODES = (0.0, 0.7, 0.25)
DEPTH = CG_ITERS
EDGE = 8
K0 = 6.0
SHIFT = 0.002
MESH = pl.DeviceIdType.MESH
F32 = jnp.float32
BF16 = jnp.bfloat16


def split(x):
    high = x.astype(BF16)
    return high, (x - high.astype(F32)).astype(BF16)


def mm(a, b):
    return jnp.dot(a, b, preferred_element_type=F32)


def total(x):
    while x.ndim > 2:
        x = jnp.sum(x, axis=0)
    return jnp.sum(jnp.sum(x, axis=0, keepdims=True), axis=1, keepdims=True)


def add(a, b):
    return b if a is None else a if b is None else a + b


def scaled(c, factor):
    return [None if v is None else v * factor for v in c]


def plus(a, b):
    n = max(len(a), len(b))
    a, b = a + [None] * (n - len(a)), b + [None] * (n - len(b))
    return [add(v, w) for v, w in zip(a, b)]


def times(c):
    out = [None] * (len(c) + 1)
    for j, v in enumerate(c):
        if v is not None:
            out[j + 1] = add(out[j + 1], v)
            node = NODES[j % BLOCK]
            if node:
                out[j] = add(out[j], v * node)
    return out


def raised(c, count):
    out = [c]
    for k in range(count):
        node = NODES[k]
        out.append(plus(times(out[-1]), scaled(out[-1], -node) if node else [None]))
    return out


def inner(a, b, gram):
    out = None
    for i, v in enumerate(a):
        if v is not None:
            row = None
            for j, w in enumerate(b):
                if w is not None:
                    row = add(row, w * gram[min(i, j), max(i, j)])
            out = add(out, v * row)
    return out


def cg_steps(r, p, gram, image_of, last):
    x = [None]
    now = inner(r, r, gram)
    for step in range(BLOCK):
        image = image_of(p)
        alpha = now / inner(p, image, gram)
        x = plus(x, scaled(p, alpha))
        r = plus(r, scaled(image, -alpha))
        if last and step == BLOCK - 1:
            break
        new = inner(r, r, gram)
        p = plus(r, scaled(p, new / now))
        now = new
    return x, r, p


def combine(c, vectors):
    out = None
    for v, w in zip(c, vectors):
        if v is not None:
            out = [v * b for b in w] if out is None else [a + v * b for a, b in zip(out, w)]
    return out


def kernel(
    n_grp, n_sub, side, coef, damaged, owners, u_ref, load_ref, cell_ref, table_any,
    inverse_any, step_ref, res_ref, tan_ref, flux_ref, kz, win, vs, ys, hx, hy, cells, seen_at, bc, chosen,
    table_ref, inverse_ref, hsend, hrecv, dsend, drecv, csend, crecv, bsend, brecv, tsend, trecv,
    fetch,
):
    g = lax.axis_index("grp")
    s = lax.axis_index("sub")
    count = n_grp * n_sub
    me = g * n_sub + s
    rows_x, rows_y, rows_z = u_ref.shape
    planes = cell_ref.shape[0]
    total_x, total_y = rows_x * n_grp, rows_y * n_sub
    win_x, win_y = kz.shape[0], kz.shape[1]
    pair = n_sub == 2
    own_y = pl.multiple_of(EDGE * s, EDGE) if pair else EDGE
    first_y = s * rows_y - own_y
    first_x = g * rows_x - DEPTH

    fetches = [
        pltpu.make_async_copy(a, b, fetch.at[i])
        for i, (a, b) in enumerate(((table_any, table_ref), (inverse_any, inverse_ref)))
    ]
    for copy in fetches:
        copy.start()
    barrier = pltpu.get_barrier_semaphore()

    def greet(k, carry):
        other = lax.rem(me + k, count)
        pl.semaphore_signal(
            barrier, inc=1, device_id={"grp": other // n_sub, "sub": lax.rem(other, n_sub)},
            device_id_type=MESH,
        )
        return carry

    lax.fori_loop(1, count, greet, 0)
    lane = lax.broadcasted_iota(jnp.int32, (1, 128), 1)
    line = lax.broadcasted_iota(jnp.int32, (1, rows_z), 1)

    def own(plane):
        if pair:
            return jnp.where(s == 0, plane[:rows_y], plane[EDGE : EDGE + rows_y])
        return plane[EDGE : EDGE + rows_y]

    def place(p):
        cell = damaged[p]
        rest = cell // rows_z
        return rest // total_y, lax.rem(rest, total_y), lax.rem(cell, rows_z)

    def row_of(values):
        out = jnp.zeros((1, 128), F32)
        for i, value in enumerate(values):
            out = out + jnp.where(lane == i, value, 0.0)
        return out

    def sample(row_x, row_y, z):
        at = lax.clamp(0, row_y, rows_y - 1)
        row = u_ref[lax.clamp(0, row_x, rows_x - 1), pl.ds(at, 1), :]
        inside = (row_x >= 0) & (row_x < rows_x) & (row_y >= 0) & (row_y < rows_y)
        keep = (line == z) & inside
        return jnp.sum(jnp.where(keep, row, 0.0), axis=1, keepdims=True)

    qx, qy, qz = place(g)
    bx, by, bz = place(lax.max(g - 1, 0))
    qx, qy, by = qx - g * rows_x, qy - s * rows_y, by - s * rows_y
    bx = jnp.where(g > 0, bx + 1 - g * rows_x, -1)
    seen = row_of([
        sample(qx, qy, qz), sample(qx + 1, qy, qz), sample(qx, qy + 1, qz),
        sample(qx, qy, qz + 1), sample(bx, by, bz),
    ])
    for i, at in enumerate((0, rows_y - 1)):
        ys[i] = u_ref[:, at : at + 1, :]

    pl.semaphore_wait(barrier, count - 1)

    g_up, g_down = lax.rem(g + 1, n_grp), lax.rem(g + n_grp - 1, n_grp)
    s_up, s_down = lax.rem(s + 1, n_sub), lax.rem(s + n_sub - 1, n_sub)

    def board(stage):
        return seen_at if stage == 0 else bc.at[stage - 1]

    def spread_start(stage, row):
        slots = board(stage)
        slots[me] = row

        def send(k, carry):
            other = lax.rem(me + k, count)
            pltpu.make_async_remote_copy(
                src_ref=slots.at[me], dst_ref=slots.at[me],
                send_sem=bsend.at[stage], recv_sem=brecv.at[stage],
                device_id={"grp": other // n_sub, "sub": lax.rem(other, n_sub)}, device_id_type=MESH,
            ).start()
            return carry

        lax.fori_loop(1, count, send, 0)

    def spread_wait(stage):
        most = board(stage).at[pl.ds(0, count - 1)]
        pltpu.make_async_copy(most, most, brecv.at[stage]).wait()
        pltpu.make_async_copy(most, most, bsend.at[stage]).wait()

    def push(moves, send, recv):
        copies = []
        for i, (a, b, to_g, to_s) in enumerate(moves):
            copy = pltpu.make_async_remote_copy(
                src_ref=a, dst_ref=b, send_sem=send.at[i], recv_sem=recv.at[i],
                device_id={"grp": to_g, "sub": to_s}, device_id_type=MESH,
            )
            copy.start()
            copies.append(copy)
        return copies

    spread_start(0, seen)
    own_cell = pl.ds(s * planes, planes)

    def cell_send(k, carry):
        to_s = lax.rem(s + k, n_sub)
        pltpu.make_async_remote_copy(
            src_ref=cell_ref, dst_ref=cells.at[own_cell], send_sem=csend, recv_sem=crecv,
            device_id={"grp": g, "sub": to_s}, device_id_type=MESH,
        ).start()
        return carry

    halo_u = push(
        (
            (u_ref.at[rows_x - 1], hx.at[0], g_up, s), (u_ref.at[0], hx.at[1], g_down, s),
            (ys.at[1], hy.at[0], g, s_up), (ys.at[0], hy.at[1], g, s_down),
        ),
        hsend, hrecv,
    )
    lax.fori_loop(1, n_sub, cell_send, 0)
    cells[own_cell] = cell_ref[...]

    def waves(at, base):
        return [jnp.cos(jnp.pi * (a + 1.0) * at / base) for a in range(4)]

    def twice(a):
        return jnp.concatenate([a] * (rows_z // 128), axis=1)

    def sheets_of(cos_y, cos_z):
        out = []
        for a in range(4):
            sheet = 0.0
            for b in range(4):
                row = coef[a + 4 * b] * cos_z[0] + coef[a + 4 * b + 16] * cos_z[1]
                sheet = sheet + row * cos_y[b]
            out.append(sheet)
        return out

    def logs(cos_x, sheets, i):
        return sum(twice(c[i : i + 1]) * sheet for c, sheet in zip(cos_x, sheets))

    at_z = line.astype(F32)
    tall = (win_x + 7) // 8 * 8
    along = lax.broadcasted_iota(jnp.int32, (tall, 128), 0)
    cos_x = waves((first_x + along).astype(F32) + 0.5, total_x)
    up = lax.broadcasted_iota(jnp.int32, (win_y, 128), 0)
    cos_y = [twice(c) for c in waves((first_y + up).astype(F32) + 0.5, total_y)]
    sheets = sheets_of(cos_y, waves(at_z + 0.5, rows_z))

    plane = (win_y, rows_z)
    y_at = lax.broadcasted_iota(jnp.int32, plane, 0)
    z_at = lax.broadcasted_iota(jnp.int32, plane, 1)
    within = None
    if not pair:
        within = ((first_y + y_at >= 0) & (first_y + y_at < total_y)).astype(F32)
    marks, spots, points = [], [], []
    for away in (-1, 0, 1):
        p = lax.clamp(0, g + away, n_grp - 1)
        x, y, z = place(p)
        valid = (g + away >= 0) & (g + away < n_grp)
        x = jnp.where(valid, x - first_x, -100)
        hit = (y_at == y - first_y) & (z_at == z)
        points.append(p)
        spots.append(x)
        marks.append(hit)
    rows_at = [jnp.where(hit, x, -100) for hit, x in zip(marks, spots)]
    marks = [jnp.where(hit, 1.0, 0.0) for hit in marks]

    def near(i):
        return 0 if i < DEPTH else 1 if i < DEPTH + rows_x else 2

    for i in range(win_x - 1):
        value = jnp.exp(0.4 * logs(cos_x, sheets, i))
        if i < DEPTH:
            value = value * (g > 0).astype(F32)
        if i >= DEPTH + rows_x:
            value = value * (g < n_grp - 1).astype(F32)
        if within is not None:
            value = value * within
        kz[i] = jnp.where(rows_at[near(i)] == i, 0.0, value)

    coarse = lax.broadcasted_iota(jnp.int32, (16, 128), 0).astype(F32)
    low = lax.broadcasted_iota(jnp.int32, (8, 128), 0).astype(F32)
    top_sheets = sheets_of([twice(c) for c in waves(low, 7)], waves(at_z, rows_z - 1))
    cos_t = waves(coarse, 15)
    top = logs(cos_t, top_sheets, 0)
    for i in range(1, 16):
        top = jnp.maximum(top, logs(cos_t, top_sheets, i))
    top = jnp.max(jnp.max(top, axis=0, keepdims=True), axis=1, keepdims=True)
    unit = 0.125 * jnp.exp(-0.4 * top)

    for copy in halo_u:
        copy.wait()
    high_x = hx[1] * (g < n_grp - 1).astype(F32)
    below, above = hy[0] * (s > 0).astype(F32), hy[1] * (s < n_sub - 1).astype(F32)
    own_at_y = lax.broadcasted_iota(jnp.int32, (rows_y, rows_z), 0)
    own_at_z = lax.broadcasted_iota(jnp.int32, (rows_y, rows_z), 1)
    u = [u_ref[i] for i in range(rows_x)] + [high_x]
    before = own(kz[DEPTH - 1]) * (u[0] - hx[0])
    for i in range(rows_x):
        k_full = kz[DEPTH + i]
        k = own(k_full)
        q0 = k * (u[i + 1] - u[i])
        q1 = k * (jnp.where(own_at_y == rows_y - 1, above[i], pltpu.roll(u[i], rows_y - 1, 0)) - u[i])
        q2 = k * (jnp.where(own_at_z == rows_z - 1, 0.0, pltpu.roll(u[i], rows_z - 1, 1)) - u[i])
        edge = k_full[EDGE - 1 : EDGE] * (s > 0).astype(F32) * (u[i][0:1] - below[i])
        out = before - q0 + jnp.where(own_at_y == 0, edge, pltpu.roll(q1, 1, 0)) - q1
        out = out + jnp.where(own_at_z == 0, 0.0, pltpu.roll(q2, 1, 1)) - q2 + SHIFT * u[i]
        win[DEPTH + i, pl.ds(own_y, rows_y), :] = load_ref[i] - out
        before = q0

    send_up, send_down = pl.ds(rows_x, DEPTH), pl.ds(DEPTH, DEPTH)
    land_up, land_down = pl.ds(0, DEPTH), pl.ds(DEPTH + rows_x, DEPTH)
    middle = pl.ds(DEPTH, rows_x)
    sides = [(pl.ds(own_y, rows_y), pl.ds(own_y, rows_y), s)]
    if pair:
        there = pl.ds(pl.multiple_of(rows_y * s, EDGE), EDGE)
        sides.append((pl.ds(EDGE, EDGE), there, s_up))
    else:
        sides.append((pl.ds(rows_y, EDGE), pl.ds(0, EDGE), s_up))
        sides.append((pl.ds(EDGE, EDGE), pl.ds(EDGE + rows_y, EDGE), s_down))
    moves = []
    for source, target, to_s in sides:
        if to_s is not s:
            moves.append((win.at[middle, source], win.at[middle, target], g, to_s))
        moves.append((win.at[send_up, source], win.at[land_up, target], g_up, to_s))
        moves.append((win.at[send_down, source], win.at[land_down, target], g_down, to_s))
    halo_r = push(moves, dsend, drecv)

    most = cells.at[pl.ds(0, planes * (n_sub - 1))]
    pltpu.make_async_copy(most, most, crecv).wait()
    pltpu.make_async_copy(most, most, csend).wait()
    for copy in fetches:
        copy.wait()
    packed = cells[...]
    turned = [packed] + [pltpu.roll(packed, i * side, 2) for i in range(1, 4)]
    set_of = lax.broadcasted_iota(jnp.int32, packed.shape, 2) // side

    def unpack(at):
        out = turned[(0 - at) % 4]
        for j in range(1, 4):
            out = jnp.where(set_of == j, turned[(j - at) % 4], out)
        return out

    def planes_of(low, high):
        parts = []
        for i in range(n_sub):
            parts += [unpack(low)[i * planes : (i + 1) * planes]]
            parts += [unpack(high)[i * planes : (i + 1) * planes]]
        return jnp.concatenate(parts, 0)

    cell_phase, cell_soften = planes_of(0, 2), planes_of(1, 3)
    spread_wait(0)

    def entry_of(row, i):
        return jnp.sum(jnp.where(lane == i, row, 0.0), axis=1, keepdims=True)

    def strain(q):
        after = lax.min(q + 1, n_grp - 1)
        row = sum(seen_at[q * n_sub + i] for i in range(n_sub))
        more = sum(seen_at[after * n_sub + i] for i in range(n_sub))
        more = jnp.where(q < n_grp - 1, more, 0.0)
        row = row + jnp.where(lane == 1, pltpu.roll(more, 125, 1), 0.0)
        values = [entry_of(row, i) for i in range(4)]
        return [v - values[0] for v in values[1:]]

    mine = sum(jnp.where(owners[q] == g, q, 0) for q in range(n_grp))
    mine = lax.min(mine, n_grp - 1)
    strength = sum(v * v for v in strain(mine))
    cond = cell_phase / (1.0 + cell_soften * strength)
    shift_k = cond - K0
    cube = (side, side, 128)
    cell_lane = lax.broadcasted_iota(jnp.int32, cube, 2)
    group = cell_lane // side
    in_group = lax.rem(cell_lane, side)

    def ahead(v, axis):
        if axis == 0:
            return jnp.concatenate([v[1:], v[:1]], 0)
        if axis == 1:
            return pltpu.roll(v, side - 1, 1)
        return jnp.where(in_group == side - 1, pltpu.roll(v, side - 1, 2), pltpu.roll(v, 127, 2))

    def behind(v, axis):
        if axis == 0:
            return jnp.concatenate([v[-1:], v[:-1]], 0)
        if axis == 1:
            return pltpu.roll(v, 1, 1)
        return jnp.where(in_group == 0, pltpu.roll(v, 129 - side, 2), pltpu.roll(v, 1, 2))

    wide = side * 8
    tz = table_ref[4, 0:128, 0:128], table_ref[5, 0:128, 0:128]
    ty = table_ref[0], table_ref[1]
    tx = table_ref[2], table_ref[3]

    def right(v):
        high, low = split(v.reshape(side * side, 128))
        return (mm(high, tz[0]) + mm(low, tz[0]) + mm(high, tz[1])).reshape(cube)

    def left(t, v):
        high, low = split(v)
        return mm(t[0], high) + mm(t[0], low) + mm(t[1], high)

    def along_y(v):
        flat = v.reshape(side * side, 128)
        parts = [left(ty, flat[i : i + wide]) for i in range(0, side * side, wide)]
        return jnp.concatenate(parts, 0).reshape(cube)

    def along_x(v):
        parts = [
            left(tx, v[:, i : i + 8].reshape(wide, 128)).reshape(side, 8, 128)
            for i in range(0, side, 8)
        ]
        return jnp.concatenate(parts, 1)

    def solve(div):
        spectrum = along_x(along_y(right(div))) * inverse_ref[...]
        return right(along_y(along_x(spectrum)))

    def div_of(phi):
        out = 0.0
        for axis in range(3):
            tau = shift_k * (ahead(phi, axis) - phi)
            out = out + tau - behind(tau, axis)
        return out

    back = jnp.where(group == 0, behind(shift_k, 0), shift_k)
    back = jnp.where(group == 1, behind(shift_k, 1), back)
    back = jnp.where(group == 2, behind(shift_k, 2), back)
    div1 = shift_k - back
    phi1 = solve(div1)
    div2 = div_of(phi1)
    phi2 = solve(div2)
    div3 = div_of(phi2)
    first, second = div1 + div2, div2 + div3
    volume = float(side**3)
    mean = total(cond) / (volume * (128 // side))
    entry = {}
    for turn in range(3):
        a = phi1 if turn == 0 else pltpu.roll(phi1, turn * side, 2)
        b = phi2 if turn == 0 else pltpu.roll(phi2, turn * side, 2)
        sums = jnp.sum(jnp.sum(a * first + b * second, axis=0), axis=0, keepdims=True)
        for j in range(turn, 3):
            value = -jnp.sum(
                jnp.where(lane // side == j, sums, 0.0), axis=1, keepdims=True
            ) / volume
            entry[j - turn, j] = entry[j, j - turn] = value + mean if turn == 0 else value
    row = jnp.zeros((1, 128), F32)
    for i in range(3):
        for j in range(3):
            row = row + jnp.where(lane == 3 * i + j, entry[i, j], 0.0)
    tan_ref[g] = row

    def tangent_send(k, carry):
        pltpu.make_async_remote_copy(
            src_ref=tan_ref.at[g], dst_ref=tan_ref.at[g], send_sem=tsend, recv_sem=trecv,
            device_id={"grp": lax.rem(g + k, n_grp), "sub": s}, device_id_type=MESH,
        ).start()
        return carry

    lax.fori_loop(1, n_grp, tangent_send, 0)

    strains = [strain(p) for p in points]
    small = SHIFT * unit
    for i in range(win_x - 1):
        kz[i] = kz[i] * unit
    for copy in halo_r:
        copy.wait()

    most = tan_ref.at[pl.ds(0, n_grp - 1)]
    pltpu.make_async_copy(most, most, trecv).wait()
    pltpu.make_async_copy(most, most, tsend).wait()

    def tensor(p):
        row = tan_ref[owners[p]]
        return {(i, j): entry_of(row, 3 * i + j) for i in range(3) for j in range(i, 3)}

    tensors = [tensor(p) for p in points]

    def rows_times(t, d):
        return [
            sum(t[min(i, j), max(i, j)] * d[j] for j in range(3)) for i in range(3)
        ]

    def next_y(v):
        return jnp.where(y_at == win_y - 1, 0.0, pltpu.roll(v, win_y - 1, 0))

    def next_z(v):
        return jnp.where(z_at == rows_z - 1, 0.0, pltpu.roll(v, rows_z - 1, 1))

    def last_y(v):
        return jnp.where(y_at == 0, 0.0, pltpu.roll(v, 1, 0))

    def last_z(v):
        return jnp.where(z_at == 0, 0.0, pltpu.roll(v, 1, 1))

    def stencil(e):
        return last_y(e[1]) + last_z(e[2]) - e[0] - e[1] - e[2]

    fixes = []
    for t, d, mark in zip(tensors, strains, marks):
        e = [v * mark for v in rows_times(t, d)]
        fixes.append((e[0], stencil(e)))

    def fix(out, i, fixes, first):
        x, center = fixes[near(i)]
        out = out + jnp.where(spots[near(i)] == i, center, 0.0)
        if i > first:
            x, center = fixes[near(i - 1)]
            out = out + jnp.where(spots[near(i - 1)] == i - 1, x, 0.0)
        return out

    for i in range(win_x):
        value = win[i]
        if i < DEPTH:
            value = value * (g > 0).astype(F32)
        if i >= DEPTH + rows_x:
            value = value * (g < n_grp - 1).astype(F32)
        if within is not None:
            value = value * within
        out = fix(jnp.zeros(plane, F32), i, fixes, 0)
        if i == DEPTH + rows_x:
            out = out * (g < n_grp - 1).astype(F32)
        vs[0, i] = value - out

    unit_tensors = [{k: v * unit for k, v in t.items()} for t in tensors]

    def advance(k):
        first, end = k, win_x - k
        node = NODES[k % BLOCK]
        keep = small - node if node else small
        fixes = []
        for t, x, mark in zip(unit_tensors, spots, marks):
            at = lax.clamp(first, x, end - 2)
            v = vs[k, at]
            e = rows_times(t, (vs[k, at + 1] - v, next_y(v) - v, next_z(v) - v))
            e = [c * mark for c in e]
            fixes.append((e[0], stencil(e)))
        v = vs[k, first]
        before = None
        for i in range(first, end - 1):
            after = vs[k, i + 1]
            weight = kz[i]
            q0 = weight * (after - v)
            if before is not None:
                q1 = weight * (next_y(v) - v)
                q2 = weight * (next_z(v) - v)
                out = before - q0 + (last_y(q1) - q1) + (last_z(q2) - q2)
                out = fix(out, i, fixes, first) + keep * v
                if i == DEPTH + rows_x:
                    out = out * (g < n_grp - 1).astype(F32)
                if within is not None:
                    out = out * within
                vs[k + 1, i] = out
            before, v = q0, after

    def own_of(k):
        return [own(vs[k, DEPTH + i]) for i in range(rows_x)]

    def dot(a, b):
        out = None
        for v, w in zip(a, b):
            out = add(out, v * w)
        parts = [
            out[i : i + 8, j : j + 128] for i in range(0, rows_y, 8) for j in range(0, rows_z, 128)
        ]
        return jnp.sum(sum(parts), axis=0, keepdims=True)

    def packed_row(parts, start=0):
        n = len(parts)
        column = jnp.sum(jnp.concatenate(parts, axis=0), axis=1, keepdims=True)
        down = lax.broadcasted_iota(jnp.int32, (n, 128), 0)
        across = lax.broadcasted_iota(jnp.int32, (n, 128), 1)
        return jnp.sum(jnp.where(across == down + start, column, 0.0), axis=0, keepdims=True)

    for k in range(BLOCK):
        advance(k)
    v = [own_of(k) for k in range(BLOCK + 1)]
    pairs = [(i, j) for i in range(BLOCK + 1) for j in range(i, BLOCK + 1)]
    spread_start(1, packed_row([dot(v[i], v[j]) for i, j in pairs]))
    for k in range(BLOCK, CG_ITERS):
        advance(k)
    for q in range(flux_ref.shape[0]):
        chosen[q] = tan_ref[owners[q]]
    v += [own_of(k) for k in range(BLOCK + 1, CG_ITERS + 1)]

    has_point = (qy >= 0) & (qy < rows_y)
    here_x = lax.clamp(DEPTH, spots[1], DEPTH + rows_x - 1)
    here_y = lax.clamp(0, qy + own_y, win_y - 1)
    next_row = lax.clamp(0, qy + own_y + 1, win_y - 1)
    at_top = qy + own_y + 1 > win_y - 1
    here = (line == qz) & has_point
    slopes = []
    for k in range(CG_ITERS):
        base = vs[k, here_x, pl.ds(here_y, 1), :]
        side_x = vs[k, here_x + 1, pl.ds(here_y, 1), :]
        side_y = jnp.where(at_top, 0.0, vs[k, here_x, pl.ds(next_row, 1), :])
        side_z = jnp.where(line == rows_z - 1, 0.0, pltpu.roll(base, rows_z - 1, 1))
        for other in (side_x, side_y, side_z):
            value = jnp.where(here, other - base, 0.0)
            slopes.append(sum(value[:, j : j + 128] for j in range(0, rows_z, 128)))
    slope_at = 64
    slope_row = packed_row(slopes, slope_at)

    spread_wait(1)
    sums = jnp.sum(bc[0], axis=0)
    gram = {key: entry_of(sums, n) for n, key in enumerate(pairs)}
    one = [jnp.ones((1, 1), F32)]
    x_c, r_c, p_c = cg_steps(one, one, gram, times, False)
    r_powers, p_powers = raised(r_c, BLOCK - 1), raised(p_c, BLOCK)
    powers = r_powers + p_powers
    basis = [combine(c, v) for c in powers]
    width = BLOCK + BLOCK + 1
    pairs = [(i, j) for i in range(width) for j in range(i, width)]
    pairs = [key for key in pairs if key not in ((BLOCK - 1,) * 2, (BLOCK - 1, width - 1), (width - 1,) * 2)]
    spread_start(2, packed_row([dot(basis[i], basis[j]) for i, j in pairs]) + slope_row)
    x = combine(x_c, v)

    def image_of(c):
        c = c + [None] * (width - len(c))
        a, b = times(c[: BLOCK - 1]), times(c[BLOCK : width - 1])
        return a + [None] * (BLOCK - len(a)) + b

    spread_wait(2)
    got = bc[1]
    sums = jnp.sum(got, axis=0)
    gram = {key: entry_of(sums, n) for n, key in enumerate(pairs)}
    start = [None] * BLOCK + one
    x2_c, r2_c, _ = cg_steps(one, start, gram, image_of, True)
    x = combine([one[0]] + x2_c, [x] + basis)
    r = combine(r2_c, basis)
    for i in range(rows_x):
        step_ref[i] = x[i] * unit
        res_ref[i] = r[i]
    whole = x_c
    for c, power in zip(x2_c, powers):
        if c is not None:
            whole = plus(whole, scaled(power, c))
    count_p = flux_ref.shape[0]
    slope = jnp.sum(got.reshape(count_p, n_sub, 1, 128), axis=1)
    spot = lax.broadcasted_iota(jnp.int32, slope.shape, 2)
    weights = jnp.zeros((1, 128), F32)
    for k in range(CG_ITERS):
        inside = (lane >= slope_at + 3 * k) & (lane < slope_at + 3 * k + 3)
        weights = weights + jnp.where(inside, whole[k] * unit, 0.0)
    slope = slope * weights[None]
    product = 0.0
    for j in range(3):
        inside = (spot >= slope_at) & (spot < slope_at + 3 * CG_ITERS)
        inside = inside & (lax.rem(spot - slope_at + 3, 3) == j)
        part = jnp.sum(jnp.where(inside, slope, 0.0), axis=2, keepdims=True)
        product = product + jnp.where((lax.rem(spot, 3) == j) & (spot < 9), chosen[...], 0.0) * part
    out = jnp.zeros_like(slope)
    for i in range(3):
        part = jnp.sum(jnp.where(spot // 3 == i, product, 0.0), axis=2, keepdims=True)
        out = out + jnp.where(spot == i, part, 0.0)
    flux_ref[...] = out


def tables(side):
    index = np.arange(side)
    angle = 2.0 * np.pi * (np.outer(index, index) % side) / side
    hartley = (np.cos(angle) + np.sin(angle)) / np.sqrt(side)
    wide = side * 8
    kinds = np.zeros((3, wide, wide), np.float64)
    kinds[0] = np.kron(np.eye(8), hartley)
    kinds[1] = np.kron(hartley, np.eye(8))
    kinds[2, :128, :128] = np.kron(np.eye(128 // side), hartley)
    kinds = kinds.astype(np.float32)
    high = kinds.astype(jnp.bfloat16)
    low = (kinds - high.astype(np.float32)).astype(jnp.bfloat16)
    table = np.stack([high, low], 1).reshape(6, wide, wide)
    line = 4.0 * np.sin(np.pi * index / side) ** 2
    lam = line[:, None, None] + line[None, :, None] + line[None, None, :]
    lam[0, 0, 0] = 1.0
    inverse = 1.0 / (K0 * lam)
    inverse[0, 0, 0] = 0.0
    return table, np.tile(inverse.astype(np.float32), (1, 1, 128 // side))


def body(displacement, load, kl_coef, damaged, owner, phase, soften):
    n_grp, n_sub = lax.axis_size("grp"), lax.axis_size("sub")
    count = n_grp * n_sub
    rows_x, rows_y, rows_z = displacement.shape
    planes = phase.shape[1]
    side = math.isqrt(phase.shape[2])
    table, inverse = tables(side)
    half = planes // 2
    cubes = [a.reshape(planes, side, side) for a in (phase, soften)]
    packed = jnp.concatenate([a[i : i + half] for i in (0, half) for a in cubes], axis=2)
    points = owner.shape[0]
    win_x = rows_x + 2 * DEPTH
    win_y = rows_y + (EDGE if n_sub == 2 else 2 * EDGE)
    moves = 5 if n_sub == 2 else 8
    vmem = pl.BlockSpec(memory_space=pltpu.VMEM)
    smem = pl.BlockSpec(memory_space=pltpu.SMEM)
    step_field, residual, rows, flux = pl.pallas_call(
        functools.partial(kernel, n_grp, n_sub, side),
        out_shape=[
            jax.ShapeDtypeStruct(displacement.shape, F32),
            jax.ShapeDtypeStruct(displacement.shape, F32),
            jax.ShapeDtypeStruct((n_grp, 1, 128), F32),
            jax.ShapeDtypeStruct((points, 1, 128), F32),
        ],
        in_specs=[smem] * 3 + [vmem] * 3 + [pl.BlockSpec(memory_space=pl.ANY)] * 2,
        out_specs=[vmem] * 4,
        scratch_shapes=[
            pltpu.VMEM((win_x, win_y, rows_z), F32),
            pltpu.VMEM((win_x, win_y, rows_z), F32),
            pltpu.VMEM((CG_ITERS + 1, win_x, win_y, rows_z), F32),
            pltpu.VMEM((2, rows_x, 1, rows_z), F32),
            pltpu.VMEM((2, rows_y, rows_z), F32),
            pltpu.VMEM((2, rows_x, 1, rows_z), F32),
            pltpu.VMEM((half * n_sub, side, 128), F32),
            pltpu.VMEM((count, 1, 128), F32),
            pltpu.VMEM((2, count, 1, 128), F32),
            pltpu.VMEM((points, 1, 128), F32),
            pltpu.VMEM(table.shape, BF16),
            pltpu.VMEM(inverse.shape, F32),
            pltpu.SemaphoreType.DMA((4,)),
            pltpu.SemaphoreType.DMA((4,)),
            pltpu.SemaphoreType.DMA((moves,)),
            pltpu.SemaphoreType.DMA((moves,)),
            pltpu.SemaphoreType.DMA,
            pltpu.SemaphoreType.DMA,
            pltpu.SemaphoreType.DMA((3,)),
            pltpu.SemaphoreType.DMA((3,)),
            pltpu.SemaphoreType.DMA,
            pltpu.SemaphoreType.DMA,
            pltpu.SemaphoreType.DMA((2,)),
        ],
        compiler_params=pltpu.CompilerParams(
            collective_id=0, has_side_effects=True, vmem_limit_bytes=48 * 2**20
        ),
    )(kl_coef, damaged, owner, displacement, load, packed, jnp.asarray(table), jnp.asarray(inverse))
    return step_field, residual, rows[:, 0, :9], flux[:, 0, :3]


def solution(mesh):
    return jax.shard_map(
        body,
        mesh=mesh,
        in_specs=(
            P("grp", "sub", None), P("grp", "sub", None), P(), P(), P(),
            P("grp", "sub", None), P("grp", "sub", None),
        ),
        out_specs=(P("grp", "sub", None), P("grp", "sub", None), P(), P()),
        check_vma=False,
    )
```

```python
import functools
import math

import jax
import jax.numpy as jnp
import numpy as np
from jax import lax
from jax.experimental import pallas as pl
from jax.experimental.pallas import tpu as pltpu
from jax.sharding import PartitionSpec as P

CG_ITERS = 6
BLOCK = CG_ITERS // 2
NODES = (0.0, 0.7, 0.25)
DEPTH = CG_ITERS
EDGE = 8
K0 = 6.0
SHIFT = 0.002
MESH = pl.DeviceIdType.MESH
F32 = jnp.float32
BF16 = jnp.bfloat16


def split(x):
    high = x.astype(BF16)
    return high, (x - high.astype(F32)).astype(BF16)


def mm(a, b):
    return jnp.dot(a, b, preferred_element_type=F32)


def total(x):
    while x.ndim > 2:
        x = jnp.sum(x, axis=0)
    return jnp.sum(jnp.sum(x, axis=0, keepdims=True), axis=1, keepdims=True)


def add(a, b):
    return b if a is None else a if b is None else a + b


def scaled(c, factor):
    return [None if v is None else v * factor for v in c]


def plus(a, b):
    n = max(len(a), len(b))
    a, b = a + [None] * (n - len(a)), b + [None] * (n - len(b))
    return [add(v, w) for v, w in zip(a, b)]


def times(c):
    out = [None] * (len(c) + 1)
    for j, v in enumerate(c):
        if v is not None:
            out[j + 1] = add(out[j + 1], v)
            node = NODES[j % BLOCK]
            if node:
                out[j] = add(out[j], v * node)
    return out


def raised(c, count):
    out = [c]
    for k in range(count):
        node = NODES[k]
        out.append(plus(times(out[-1]), scaled(out[-1], -node) if node else [None]))
    return out


def inner(a, b, gram):
    out = None
    for i, v in enumerate(a):
        if v is not None:
            row = None
            for j, w in enumerate(b):
                if w is not None:
                    row = add(row, w * gram[min(i, j), max(i, j)])
            out = add(out, v * row)
    return out


def cg_steps(r, p, gram, image_of, last):
    x = [None]
    now = inner(r, r, gram)
    for step in range(BLOCK):
        image = image_of(p)
        alpha = now / inner(p, image, gram)
        x = plus(x, scaled(p, alpha))
        r = plus(r, scaled(image, -alpha))
        if last and step == BLOCK - 1:
            break
        new = inner(r, r, gram)
        p = plus(r, scaled(p, new / now))
        now = new
    return x, r, p


def combine(c, vectors):
    out = None
    for v, w in zip(c, vectors):
        if v is not None:
            out = [v * b for b in w] if out is None else [a + v * b for a, b in zip(out, w)]
    return out


def kernel(
    n_grp, n_sub, side, coef, damaged, owners, u_any, load_any, phase_any, soften_any, table_any,
    turn_any, inverse_any, field_ref, small_ref, tan_ref, u_ref, load_ref, kz, win, vs, ys,
    hx, hy, cells, seen_at, bc, chosen, table_ref, turn_ref, inverse_ref, hsend, hrecv, dsend,
    drecv, csend, crecv, bsend, brecv, tsend, trecv, fetch, gather,
):
    g = lax.axis_index("grp")
    s = lax.axis_index("sub")
    count = n_grp * n_sub
    me = g * n_sub + s
    rows_x, rows_y, rows_z = u_ref.shape
    planes = phase_any.shape[1]
    per = 128 // side
    wide = side * 8
    total_x, total_y = rows_x * n_grp, rows_y * n_sub
    win_x, win_y = kz.shape[0], kz.shape[1]
    pair = n_sub == 2
    own_y = pl.multiple_of(EDGE * s, EDGE) if pair else EDGE
    first_y = s * rows_y - own_y
    first_x = g * rows_x - DEPTH

    fetches = [
        pltpu.make_async_copy(a, b, fetch.at[i])
        for i, (a, b) in enumerate((
            (u_any, u_ref), (load_any, load_ref), (table_any, table_ref), (turn_any, turn_ref),
            (inverse_any, inverse_ref),
        ))
    ]
    barrier = pltpu.get_barrier_semaphore()
    fetches[0].start()
    own_cell = pl.ds(s * planes, planes)
    for i, ref in enumerate((phase_any, soften_any)):
        for j in range(side // per):
            pltpu.make_async_copy(
                ref.at[0, :, pl.ds(128 * j, 128)], cells.at[i, own_cell, j, :], gather.at[i]
            ).start()

    def greet(k, carry):
        other = lax.rem(me + k, count)
        pl.semaphore_signal(
            barrier, inc=1, device_id={"grp": other // n_sub, "sub": lax.rem(other, n_sub)},
            device_id_type=MESH,
        )
        return carry

    lax.fori_loop(1, count, greet, 0)
    for copy in fetches[1:]:
        copy.start()
    lane = lax.broadcasted_iota(jnp.int32, (1, 128), 1)
    line = lax.broadcasted_iota(jnp.int32, (1, rows_z), 1)

    def place(p):
        cell = damaged[p]
        rest = cell // rows_z
        return rest // total_y, lax.rem(rest, total_y), lax.rem(cell, rows_z)

    def row_of(values):
        out = jnp.zeros((1, 128), F32)
        for i, value in enumerate(values):
            out = out + jnp.where(lane == i, value, 0.0)
        return out

    def sample(row_x, row_y, z):
        at = lax.clamp(0, row_y, rows_y - 1)
        row = u_ref[lax.clamp(0, row_x, rows_x - 1), pl.ds(at, 1), :]
        inside = (row_x >= 0) & (row_x < rows_x) & (row_y >= 0) & (row_y < rows_y)
        keep = (line == z) & inside
        return jnp.sum(jnp.where(keep, row, 0.0), axis=1, keepdims=True)

    fetches[0].wait()
    qx, qy, qz = place(g)
    bx, by, bz = place(lax.max(g - 1, 0))
    qx, qy, by = qx - g * rows_x, qy - s * rows_y, by - s * rows_y
    bx = jnp.where(g > 0, bx + 1 - g * rows_x, -1)
    seen = row_of([
        sample(qx, qy, qz), sample(qx + 1, qy, qz), sample(qx, qy + 1, qz),
        sample(qx, qy, qz + 1), sample(bx, by, bz),
    ])
    for i, at in enumerate((0, rows_y - 1)):
        ys[i] = u_ref[:, at : at + 1, :]
    for i in range(2):
        block = cells.at[i, pl.ds(0, planes)]
        pltpu.make_async_copy(block, block, gather.at[i]).wait()

    pl.semaphore_wait(barrier, count - 1)

    g_up, g_down = lax.rem(g + 1, n_grp), lax.rem(g + n_grp - 1, n_grp)
    s_up, s_down = lax.rem(s + 1, n_sub), lax.rem(s + n_sub - 1, n_sub)

    def board(stage):
        return seen_at if stage == 0 else bc.at[stage - 1]

    def spread_start(stage, row):
        slots = board(stage)
        slots[me] = row

        def send(k, carry):
            other = lax.rem(me + k, count)
            pltpu.make_async_remote_copy(
                src_ref=slots.at[me], dst_ref=slots.at[me],
                send_sem=bsend.at[stage], recv_sem=brecv.at[stage],
                device_id={"grp": other // n_sub, "sub": lax.rem(other, n_sub)}, device_id_type=MESH,
            ).start()
            return carry

        lax.fori_loop(1, count, send, 0)

    def spread_wait(stage):
        most = board(stage).at[pl.ds(0, count - 1)]
        pltpu.make_async_copy(most, most, brecv.at[stage]).wait()
        pltpu.make_async_copy(most, most, bsend.at[stage]).wait()

    def push(moves, send, recv):
        copies = []
        for i, (a, b, to_g, to_s) in enumerate(moves):
            copy = pltpu.make_async_remote_copy(
                src_ref=a, dst_ref=b, send_sem=send.at[i], recv_sem=recv.at[i],
                device_id={"grp": to_g, "sub": to_s}, device_id_type=MESH,
            )
            copy.start()
            copies.append(copy)
        return copies

    spread_start(0, seen)
    def cell_send(k, carry):
        to_s = lax.rem(s + k, n_sub)
        for i in range(2):
            pltpu.make_async_remote_copy(
                src_ref=cells.at[i, own_cell], dst_ref=cells.at[i, own_cell], send_sem=csend.at[i],
                recv_sem=crecv.at[i], device_id={"grp": g, "sub": to_s}, device_id_type=MESH,
            ).start()
        return carry

    halo_u = push(
        (
            (u_ref.at[rows_x - 1], hx.at[0], g_up, s), (u_ref.at[0], hx.at[1], g_down, s),
            (ys.at[1], hy.at[0], g, s_up), (ys.at[0], hy.at[1], g, s_down),
        ),
        hsend, hrecv,
    )
    lax.fori_loop(1, n_sub, cell_send, 0)

    def waves(at, base):
        return [jnp.cos(jnp.pi * (a + 1.0) * at / base) for a in range(4)]

    def twice(a):
        return jnp.concatenate([a] * (rows_z // 128), axis=1)

    def sheets_of(cos_y, cos_z):
        out = []
        for a in range(4):
            sheet = 0.0
            for b in range(4):
                row = coef[a + 4 * b] * cos_z[0] + coef[a + 4 * b + 16] * cos_z[1]
                sheet = sheet + row * cos_y[b]
            out.append(sheet)
        return out

    def logs(cos_x, sheets, i):
        return sum(twice(c[i : i + 1]) * sheet for c, sheet in zip(cos_x, sheets))

    at_z = line.astype(F32)
    tall = (win_x + 7) // 8 * 8
    along = lax.broadcasted_iota(jnp.int32, (tall, 128), 0)
    cos_x = waves((first_x + along).astype(F32) + 0.5, total_x)
    up = lax.broadcasted_iota(jnp.int32, (win_y, 128), 0)
    cos_y = [twice(c) for c in waves((first_y + up).astype(F32) + 0.5, total_y)]
    sheets = sheets_of(cos_y, waves(at_z + 0.5, rows_z))

    plane = (win_y, rows_z)
    y_at = lax.broadcasted_iota(jnp.int32, plane, 0)
    z_at = lax.broadcasted_iota(jnp.int32, plane, 1)
    within = None
    if not pair:
        within = ((first_y + y_at >= 0) & (first_y + y_at < total_y)).astype(F32)
    marks, spots, points = [], [], []
    for away in (-1, 0, 1):
        p = lax.clamp(0, g + away, n_grp - 1)
        x, y, z = place(p)
        valid = (g + away >= 0) & (g + away < n_grp)
        x = jnp.where(valid, x - first_x, -100)
        hit = (y_at == y - first_y) & (z_at == z)
        points.append(p)
        spots.append(x)
        marks.append(hit)
    rows_at = [jnp.where(hit, x, -100) for hit, x in zip(marks, spots)]
    marks = [jnp.where(hit, 1.0, 0.0) for hit in marks]

    def near(i):
        return 0 if i < DEPTH else 1 if i < DEPTH + rows_x else 2

    for i in range(win_x - 1):
        value = jnp.exp(0.4 * logs(cos_x, sheets, i))
        if i < DEPTH:
            value = value * (g > 0).astype(F32)
        if i >= DEPTH + rows_x:
            value = value * (g < n_grp - 1).astype(F32)
        if within is not None:
            value = value * within
        kz[i] = jnp.where(rows_at[near(i)] == i, 0.0, value)

    coarse = lax.broadcasted_iota(jnp.int32, (16, 128), 0).astype(F32)
    low = lax.broadcasted_iota(jnp.int32, (8, 128), 0).astype(F32)
    top_sheets = sheets_of([twice(c) for c in waves(low, 7)], waves(at_z, rows_z - 1))
    cos_t = waves(coarse, 15)
    top = logs(cos_t, top_sheets, 0)
    for i in range(1, 16):
        top = jnp.maximum(top, logs(cos_t, top_sheets, i))
    top = jnp.max(jnp.max(top, axis=0, keepdims=True), axis=1, keepdims=True)
    unit = 0.125 * jnp.exp(-0.4 * top)

    for copy in halo_u:
        copy.wait()
    fetches[1].wait()
    high_x = hx[1] * (g < n_grp - 1).astype(F32)
    below, above = hy[0] * (s > 0).astype(F32), hy[1] * (s < n_sub - 1).astype(F32)
    own_at_y = lax.broadcasted_iota(jnp.int32, (rows_y, rows_z), 0)
    own_at_z = lax.broadcasted_iota(jnp.int32, (rows_y, rows_z), 1)
    u = [u_ref[i] for i in range(rows_x)] + [high_x]
    before = kz[DEPTH - 1, pl.ds(own_y, rows_y), :] * (u[0] - hx[0])
    for i in range(rows_x):
        k = kz[DEPTH + i, pl.ds(own_y, rows_y), :]
        q0 = k * (u[i + 1] - u[i])
        q1 = k * (jnp.where(own_at_y == rows_y - 1, above[i], pltpu.roll(u[i], rows_y - 1, 0)) - u[i])
        q2 = k * (jnp.where(own_at_z == rows_z - 1, 0.0, pltpu.roll(u[i], rows_z - 1, 1)) - u[i])
        edge = kz[DEPTH + i, EDGE - 1 : EDGE, :] * (s > 0).astype(F32) * (u[i][0:1] - below[i])
        out = before - q0 + jnp.where(own_at_y == 0, edge, pltpu.roll(q1, 1, 0)) - q1
        out = out + jnp.where(own_at_z == 0, 0.0, pltpu.roll(q2, 1, 1)) - q2 + SHIFT * u[i]
        win[DEPTH + i, pl.ds(own_y, rows_y), :] = load_ref[i] - out
        before = q0

    send_up, send_down = pl.ds(rows_x, DEPTH), pl.ds(DEPTH, DEPTH)
    land_up, land_down = pl.ds(0, DEPTH), pl.ds(DEPTH + rows_x, DEPTH)
    middle = pl.ds(DEPTH, rows_x)
    sides = [(pl.ds(own_y, rows_y), pl.ds(own_y, rows_y), s)]
    if pair:
        there = pl.ds(pl.multiple_of(rows_y * s, EDGE), EDGE)
        sides.append((pl.ds(EDGE, EDGE), there, s_up))
    else:
        sides.append((pl.ds(rows_y, EDGE), pl.ds(0, EDGE), s_up))
        sides.append((pl.ds(EDGE, EDGE), pl.ds(EDGE + rows_y, EDGE), s_down))
    moves = []
    for source, target, to_s in sides:
        if to_s is not s:
            moves.append((win.at[middle, source], win.at[middle, target], g, to_s))
        moves.append((win.at[send_up, source], win.at[land_up, target], g_up, to_s))
        moves.append((win.at[send_down, source], win.at[land_down, target], g_down, to_s))
    halo_r = push(moves, dsend, drecv)

    for i in range(2):
        most = cells.at[i, pl.ds(0, planes * (n_sub - 1))]
        pltpu.make_async_copy(most, most, crecv.at[i]).wait()
        pltpu.make_async_copy(most, most, csend.at[i]).wait()
    for copy in fetches[2:]:
        copy.wait()
    spread_wait(0)

    def entry_of(row, i):
        return jnp.sum(jnp.where(lane == i, row, 0.0), axis=1, keepdims=True)

    def strain(q):
        after = lax.min(q + 1, n_grp - 1)
        row = sum(seen_at[q * n_sub + i] for i in range(n_sub))
        more = sum(seen_at[after * n_sub + i] for i in range(n_sub))
        more = jnp.where(q < n_grp - 1, more, 0.0)
        row = row + jnp.where(lane == 1, pltpu.roll(more, 125, 1), 0.0)
        values = [entry_of(row, i) for i in range(4)]
        return [v - values[0] for v in values[1:]]

    mine = sum(jnp.where(owners[q] == g, q, 0) for q in range(n_grp))
    mine = lax.min(mine, n_grp - 1)
    strength = sum(v * v for v in strain(mine))
    cond = cells[0] / (1.0 + cells[1] * strength)
    turned = [cond - K0]
    turned += [pltpu.roll(turned[0], i * side, 2) for i in range(1, per)]
    cube = (side, side, 128)
    cell_lane = lax.broadcasted_iota(jnp.int32, (1, 8, 128), 2)
    group = cell_lane // side
    in_group = lax.rem(cell_lane, side)
    parts = []
    for t in range(per):
        part = turned[(0 - t) % per]
        for j in range(1, per):
            part = jnp.where(group == j, turned[(j - t) % per], part)
        parts.append(part)
    shift_k = parts

    def ahead(v, axis):
        if axis == 0:
            return [jnp.concatenate([a[1:], a[:1]], 0) for a in v]
        if axis == 1:
            return v[1:] + [pltpu.roll(v[0], 7, 1)]
        return [
            jnp.where(in_group == side - 1, pltpu.roll(a, side - 1, 2), pltpu.roll(a, 127, 2))
            for a in v
        ]

    def behind(v, axis):
        if axis == 0:
            return [jnp.concatenate([a[-1:], a[:-1]], 0) for a in v]
        if axis == 1:
            return [pltpu.roll(v[-1], 1, 1)] + v[:-1]
        return [
            jnp.where(in_group == 0, pltpu.roll(a, 129 - side, 2), pltpu.roll(a, 1, 2)) for a in v
        ]

    def right(v):
        high, low = split(v)
        both = mm(jnp.concatenate([high, low], axis=1), turn_ref[...])
        return both[:, :128] + both[:, 128:]

    def left(t, v):
        high, low = split(v)
        both = mm(table_ref[t], high)
        return both[:wide] + both[wide:] + mm(table_ref[t, :wide], low)

    def halves(a, b, t):
        out = left(t, jnp.concatenate([a, b], axis=1))
        return out[:, :128], out[:, 128:]

    def along_z(v):
        return [right(a.reshape(wide, 128)).reshape(side, 8, 128) for a in v]

    def along_x(v):
        out = []
        for i in range(0, per, 2):
            for a in halves(v[i].reshape(wide, 128), v[i + 1].reshape(wide, 128), 1):
                out.append(a.reshape(side, 8, 128))
        return out

    def along_y(v):
        out = [[] for _ in range(per)]
        for i in range(0, side, 16):
            blocks = [
                jnp.concatenate([a[j : j + 8] for a in v], axis=1).reshape(wide, 128)
                for j in (i, i + 8)
            ]
            for block in halves(blocks[0], blocks[1], 0):
                block = block.reshape(8, side, 128)
                for t in range(per):
                    out[t].append(block[:, 8 * t : 8 * t + 8])
        return [jnp.concatenate(a, axis=0) for a in out]

    def solve(div):
        spectrum = along_x(along_y(along_z(div)))
        spectrum = [a * inverse_ref[:, 8 * t : 8 * t + 8] for t, a in enumerate(spectrum)]
        return along_z(along_y(along_x(spectrum)))

    def div_of(phi):
        out = [0.0] * per
        for axis in range(3):
            tau = [k * (a - b) for k, a, b in zip(shift_k, ahead(phi, axis), phi)]
            out = [o + a - b for o, a, b in zip(out, tau, behind(tau, axis))]
        return out

    backs = [behind(shift_k, axis) for axis in range(3)]
    div1 = []
    for t in range(per):
        back = jnp.where(group == 0, backs[0][t], shift_k[t])
        back = jnp.where(group == 1, backs[1][t], back)
        div1.append(shift_k[t] - jnp.where(group == 2, backs[2][t], back))
    phi1 = solve(div1)
    div2 = div_of(phi1)
    phi2 = solve(div2)
    div3 = div_of(phi2)
    first = [a + b for a, b in zip(div1, div2)]
    second = [a + b for a, b in zip(div2, div3)]
    volume = float(side**3)
    mean = total(cond) / volume
    entry = {}
    for turn in range(3):
        sums = 0.0
        for t in range(per):
            a = phi1[t] if turn == 0 else pltpu.roll(phi1[t], turn * side, 2)
            b = phi2[t] if turn == 0 else pltpu.roll(phi2[t], turn * side, 2)
            sums = sums + jnp.sum(a * first[t] + b * second[t], axis=0)
        sums = jnp.sum(sums, axis=0, keepdims=True)
        for j in range(turn, 3):
            value = -jnp.sum(
                jnp.where(lane // side == j, sums, 0.0), axis=1, keepdims=True
            ) / volume
            entry[j - turn, j] = entry[j, j - turn] = value + mean if turn == 0 else value
    row = jnp.zeros((1, 128), F32)
    for i in range(3):
        for j in range(3):
            row = row + jnp.where(lane == 3 * i + j, entry[i, j], 0.0)
    tan_ref[g] = row

    def tangent_send(k, carry):
        pltpu.make_async_remote_copy(
            src_ref=tan_ref.at[g], dst_ref=tan_ref.at[g], send_sem=tsend, recv_sem=trecv,
            device_id={"grp": lax.rem(g + k, n_grp), "sub": s}, device_id_type=MESH,
        ).start()
        return carry

    lax.fori_loop(1, n_grp, tangent_send, 0)

    strains = [strain(p) for p in points]
    small = SHIFT * unit
    for i in range(win_x - 1):
        kz[i] = kz[i] * unit
    for copy in halo_r:
        copy.wait()

    most = tan_ref.at[pl.ds(0, n_grp - 1)]
    pltpu.make_async_copy(most, most, trecv).wait()
    pltpu.make_async_copy(most, most, tsend).wait()

    def tensor(p):
        row = tan_ref[owners[p]]
        return {(i, j): entry_of(row, 3 * i + j) for i in range(3) for j in range(i, 3)}

    tensors = [tensor(p) for p in points]

    def rows_times(t, d):
        return [
            sum(t[min(i, j), max(i, j)] * d[j] for j in range(3)) for i in range(3)
        ]

    def next_y(v):
        return jnp.where(y_at == win_y - 1, 0.0, pltpu.roll(v, win_y - 1, 0))

    def next_z(v):
        return jnp.where(z_at == rows_z - 1, 0.0, pltpu.roll(v, rows_z - 1, 1))

    def last_y(v):
        return jnp.where(y_at == 0, 0.0, pltpu.roll(v, 1, 0))

    def last_z(v):
        return jnp.where(z_at == 0, 0.0, pltpu.roll(v, 1, 1))

    def stencil(e):
        return last_y(e[1]) + last_z(e[2]) - e[0] - e[1] - e[2]

    fixes = []
    for t, d, mark in zip(tensors, strains, marks):
        e = [v * mark for v in rows_times(t, d)]
        fixes.append((e[0], stencil(e)))

    def fix(out, i, fixes, first):
        x, center = fixes[near(i)]
        out = out + jnp.where(spots[near(i)] == i, center, 0.0)
        if i > first:
            x, center = fixes[near(i - 1)]
            out = out + jnp.where(spots[near(i - 1)] == i - 1, x, 0.0)
        return out

    for i in range(win_x):
        value = win[i]
        if i < DEPTH:
            value = value * (g > 0).astype(F32)
        if i >= DEPTH + rows_x:
            value = value * (g < n_grp - 1).astype(F32)
        if within is not None:
            value = value * within
        out = fix(jnp.zeros(plane, F32), i, fixes, 0)
        if i == DEPTH + rows_x:
            out = out * (g < n_grp - 1).astype(F32)
        vs[0, i] = value - out

    unit_tensors = [{k: v * unit for k, v in t.items()} for t in tensors]

    sub_at = lax.broadcasted_iota(jnp.int32, (8, 128), 0)
    lane_at = lax.broadcasted_iota(jnp.int32, (8, 128), 1)
    tiles_y, tiles_z = win_y // 8, rows_z // 128
    cells_at = [(a, b) for a in range(tiles_y) for b in range(tiles_z)]

    def tiles_of(ref, *at):
        return {
            (a, b): ref[(*at, pl.ds(8 * a, 8), pl.ds(128 * b, 128))] for a, b in cells_at
        }

    def cut(v):
        return {(a, b): v[8 * a : 8 * a + 8, 128 * b : 128 * b + 128] for a, b in cells_at}

    def moved(v, axis, by):
        size = (8, 128)[axis]
        rolled = {key: pltpu.roll(w, by % size, axis) for key, w in v.items()}
        edge = (sub_at, lane_at)[axis] == (size - 1 if by < 0 else 0)
        out = {}
        for a, b in v:
            other = (a - by, b) if axis == 0 else (a, b - by)
            out[a, b] = jnp.where(edge, rolled.get(other, 0.0), rolled[a, b])
        return out

    def advance(k):
        first, end = k, win_x - k
        node = NODES[k % BLOCK]
        keep = small - node if node else small
        fixes = []
        for t, x, mark in zip(unit_tensors, spots, marks):
            at = lax.clamp(first, x, end - 2)
            v = vs[k, at]
            e = rows_times(t, (vs[k, at + 1] - v, next_y(v) - v, next_z(v) - v))
            e = [c * mark for c in e]
            fixes.append((cut(e[0]), cut(stencil(e))))
        v = tiles_of(vs, k, first)
        before = None
        for i in range(first, end - 1):
            after = tiles_of(vs, k, i + 1)
            weight = tiles_of(kz, i)
            q0 = {c: weight[c] * (after[c] - v[c]) for c in cells_at}
            if before is not None:
                up_y, up_z = moved(v, 0, -1), moved(v, 1, -1)
                q1 = {c: weight[c] * (up_y[c] - v[c]) for c in cells_at}
                q2 = {c: weight[c] * (up_z[c] - v[c]) for c in cells_at}
                low_y, low_z = moved(q1, 0, 1), moved(q2, 1, 1)
                now, past = near(i), near(i - 1)
                for a, b in cells_at:
                    c = a, b
                    extra = jnp.where(spots[past] == i - 1, fixes[past][0][c], 0.0)
                    extra = jnp.where(spots[now] == i, fixes[now][1][c], extra)
                    if now != past:
                        extra = extra + jnp.where(
                            (spots[now] == i) & (spots[past] == i - 1), fixes[past][0][c], 0.0
                        )
                    out = (before[c] - q0[c]) + (low_y[c] - q1[c])
                    out = out + ((low_z[c] - q2[c]) + (extra + keep * v[c]))
                    if i == DEPTH + rows_x:
                        out = out * (g < n_grp - 1).astype(F32)
                    if within is not None:
                        out = out * within[8 * a : 8 * a + 8, 128 * b : 128 * b + 128]
                    vs[k + 1, i, pl.ds(8 * a, 8), pl.ds(128 * b, 128)] = out
            before, v = q0, after

    def own_of(k):
        return [vs[k, DEPTH + i, pl.ds(own_y, rows_y), :] for i in range(rows_x)]

    def dot(a, b):
        out = None
        for v, w in zip(a, b):
            out = add(out, v * w)
        parts = [
            out[i : i + 8, j : j + 128] for i in range(0, rows_y, 8) for j in range(0, rows_z, 128)
        ]
        return jnp.sum(sum(parts), axis=0, keepdims=True)

    def packed_row(parts, start=0):
        n = len(parts)
        column = jnp.sum(jnp.concatenate(parts, axis=0), axis=1, keepdims=True)
        down = lax.broadcasted_iota(jnp.int32, (n, 128), 0)
        across = lax.broadcasted_iota(jnp.int32, (n, 128), 1)
        return jnp.sum(jnp.where(across == down + start, column, 0.0), axis=0, keepdims=True)

    for k in range(BLOCK):
        advance(k)
    v = [own_of(k) for k in range(BLOCK + 1)]
    pairs = [(i, j) for i in range(BLOCK + 1) for j in range(i, BLOCK + 1)]
    spread_start(1, packed_row([dot(v[i], v[j]) for i, j in pairs]))
    for k in range(BLOCK, CG_ITERS):
        advance(k)
    for q in range(n_grp):
        chosen[q] = tan_ref[owners[q]]
    v += [own_of(k) for k in range(BLOCK + 1, CG_ITERS + 1)]

    has_point = (qy >= 0) & (qy < rows_y)
    here_x = lax.clamp(DEPTH, spots[1], DEPTH + rows_x - 1)
    here_y = lax.clamp(0, qy + own_y, win_y - 1)
    next_row = lax.clamp(0, qy + own_y + 1, win_y - 1)
    at_top = qy + own_y + 1 > win_y - 1
    here = (line == qz) & has_point
    slopes = []
    for k in range(CG_ITERS):
        base = vs[k, here_x, pl.ds(here_y, 1), :]
        side_x = vs[k, here_x + 1, pl.ds(here_y, 1), :]
        side_y = jnp.where(at_top, 0.0, vs[k, here_x, pl.ds(next_row, 1), :])
        side_z = jnp.where(line == rows_z - 1, 0.0, pltpu.roll(base, rows_z - 1, 1))
        for other in (side_x, side_y, side_z):
            value = jnp.where(here, other - base, 0.0)
            slopes.append(sum(value[:, j : j + 128] for j in range(0, rows_z, 128)))
    slope_at = 64
    slope_row = packed_row(slopes, slope_at)

    spread_wait(1)
    sums = jnp.sum(bc[0], axis=0)
    gram = {key: entry_of(sums, n) for n, key in enumerate(pairs)}
    one = [jnp.ones((1, 1), F32)]
    x_c, r_c, p_c = cg_steps(one, one, gram, times, False)
    r_powers, p_powers = raised(r_c, BLOCK - 1), raised(p_c, BLOCK)
    powers = r_powers + p_powers
    basis = [combine(c, v) for c in powers]
    width = BLOCK + BLOCK + 1
    pairs = [(i, j) for i in range(width) for j in range(i, width)]
    pairs = [key for key in pairs if key not in ((BLOCK - 1,) * 2, (BLOCK - 1, width - 1), (width - 1,) * 2)]
    spread_start(2, packed_row([dot(basis[i], basis[j]) for i, j in pairs]) + slope_row)
    x = combine(x_c, v)

    def image_of(c):
        c = c + [None] * (width - len(c))
        a, b = times(c[: BLOCK - 1]), times(c[BLOCK : width - 1])
        return a + [None] * (BLOCK - len(a)) + b

    spread_wait(2)
    got = bc[1]
    sums = jnp.sum(got, axis=0)
    gram = {key: entry_of(sums, n) for n, key in enumerate(pairs)}
    start = [None] * BLOCK + one
    x2_c, r2_c, _ = cg_steps(one, start, gram, image_of, True)
    x = combine([one[0]] + x2_c, [x] + basis)
    r = combine(r2_c, basis)
    for i in range(rows_x):
        field_ref[0, i] = x[i] * unit
        field_ref[1, i] = r[i]
    whole = x_c
    for c, power in zip(x2_c, powers):
        if c is not None:
            whole = plus(whole, scaled(power, c))
    slope = jnp.sum(got.reshape(n_grp, n_sub, 1, 128), axis=1)
    spot = lax.broadcasted_iota(jnp.int32, slope.shape, 2)
    weights = jnp.zeros((1, 128), F32)
    for k in range(CG_ITERS):
        inside = (lane >= slope_at + 3 * k) & (lane < slope_at + 3 * k + 3)
        weights = weights + jnp.where(inside, whole[k] * unit, 0.0)
    slope = slope * weights[None]
    product = 0.0
    for j in range(3):
        inside = (spot >= slope_at) & (spot < slope_at + 3 * CG_ITERS)
        inside = inside & (lax.rem(spot - slope_at + 3, 3) == j)
        part = jnp.sum(jnp.where(inside, slope, 0.0), axis=2, keepdims=True)
        product = product + jnp.where((lax.rem(spot, 3) == j) & (spot < 9), chosen[...], 0.0) * part
    out = jnp.zeros_like(slope)
    for i in range(3):
        part = jnp.sum(jnp.where(spot // 3 == i, product, 0.0), axis=2, keepdims=True)
        out = out + jnp.where(spot == 9 + i, part, 0.0)
    for q in range(n_grp):
        small_ref[q : q + 1] = jnp.where(lane < 9, tan_ref[q], out[q])


def tables(side):
    index = np.arange(side)
    per = 128 // side
    place = np.arange(side).reshape(side // per, per).T.reshape(-1)
    angle = 2.0 * np.pi * (np.outer(index, index) % side) / side
    hartley = (np.cos(angle) + np.sin(angle)) / np.sqrt(side)

    def halves(a):
        a = a.astype(np.float32)
        high = a.astype(jnp.bfloat16)
        return high, (a - high.astype(np.float32)).astype(jnp.bfloat16)

    kinds = np.kron(np.eye(8), hartley[place][:, place]), np.kron(hartley, np.eye(8))
    table = np.stack([np.concatenate(halves(a), axis=0) for a in kinds])
    high, low = halves(np.kron(np.eye(per), hartley))
    turn = np.block([[high, low], [high, np.zeros_like(low)]])
    line = 4.0 * np.sin(np.pi * index / side) ** 2
    lam = line[:, None, None] + line[None, place, None] + line[None, None, :]
    lam[0, 0, 0] = 1.0
    inverse = 1.0 / (K0 * lam)
    inverse[0, 0, 0] = 0.0
    return table, turn, np.tile(inverse.astype(np.float32), (1, 1, per))


def body(displacement, load, kl_coef, damaged, owner, phase, soften):
    n_grp, n_sub = lax.axis_size("grp"), lax.axis_size("sub")
    count = n_grp * n_sub
    rows_x, rows_y, rows_z = displacement.shape
    planes = phase.shape[1]
    side = math.isqrt(phase.shape[2])
    table, turn, inverse = tables(side)
    points = owner.shape[0]
    win_x = rows_x + 2 * DEPTH
    win_y = rows_y + (EDGE if n_sub == 2 else 2 * EDGE)
    moves = 5 if n_sub == 2 else 8
    vmem = pl.BlockSpec(memory_space=pltpu.VMEM)
    smem = pl.BlockSpec(memory_space=pltpu.SMEM)
    fields, small = pl.pallas_call(
        functools.partial(kernel, n_grp, n_sub, side),
        out_shape=[
            jax.ShapeDtypeStruct((2, *displacement.shape), F32),
            jax.ShapeDtypeStruct((points, 128), F32),
        ],
        in_specs=[smem] * 3 + [pl.BlockSpec(memory_space=pl.ANY)] * 7,
        out_specs=[vmem] * 2,
        scratch_shapes=[
            pltpu.VMEM((n_grp, 1, 128), F32),
            pltpu.VMEM(displacement.shape, F32),
            pltpu.VMEM(displacement.shape, F32),
            pltpu.VMEM((win_x, win_y, rows_z), F32),
            pltpu.VMEM((win_x, win_y, rows_z), F32),
            pltpu.VMEM((CG_ITERS + 1, win_x, win_y, rows_z), F32),
            pltpu.VMEM((2, rows_x, 1, rows_z), F32),
            pltpu.VMEM((2, rows_y, rows_z), F32),
            pltpu.VMEM((2, rows_x, 1, rows_z), F32),
            pltpu.VMEM((2, side, side * side // 128, 128), F32),
            pltpu.VMEM((count, 1, 128), F32),
            pltpu.VMEM((2, count, 1, 128), F32),
            pltpu.VMEM((points, 1, 128), F32),
            pltpu.VMEM(table.shape, BF16),
            pltpu.VMEM(turn.shape, BF16),
            pltpu.VMEM(inverse.shape, F32),
            pltpu.SemaphoreType.DMA((4,)),
            pltpu.SemaphoreType.DMA((4,)),
            pltpu.SemaphoreType.DMA((moves,)),
            pltpu.SemaphoreType.DMA((moves,)),
            pltpu.SemaphoreType.DMA((2,)),
            pltpu.SemaphoreType.DMA((2,)),
            pltpu.SemaphoreType.DMA((3,)),
            pltpu.SemaphoreType.DMA((3,)),
            pltpu.SemaphoreType.DMA,
            pltpu.SemaphoreType.DMA,
            pltpu.SemaphoreType.DMA((5,)),
            pltpu.SemaphoreType.DMA((2,)),
        ],
        compiler_params=pltpu.CompilerParams(collective_id=0, has_side_effects=True),
    )(kl_coef, damaged, owner, displacement, load, phase, soften, jnp.asarray(table),
      jnp.asarray(turn), jnp.asarray(inverse))
    return fields[0], fields[1], small[:, :9], small[:, 9:12]


def solution(mesh):
    return jax.shard_map(
        body,
        mesh=mesh,
        in_specs=(
            P("grp", "sub", None), P("grp", "sub", None), P(), P(), P(),
            P("grp", "sub", None), P("grp", "sub", None),
        ),
        out_specs=(P("grp", "sub", None), P("grp", "sub", None), P(), P()),
        check_vma=False,
    )
```

```python
import functools
import math

import jax
import jax.numpy as jnp
import numpy as np
from jax import lax
from jax.experimental import pallas as pl
from jax.experimental.pallas import tpu as pltpu
from jax.sharding import PartitionSpec as P

CG_ITERS = 6
BLOCK = CG_ITERS // 2
NODES = (0.0, 0.7, 0.25)
DEPTH = CG_ITERS
EDGE = 8
K0 = 6.0
SHIFT = 0.002
MESH = pl.DeviceIdType.MESH
F32 = jnp.float32
BF16 = jnp.bfloat16


def split(x):
    high = x.astype(BF16)
    return high, (x - high.astype(F32)).astype(BF16)


def mm(a, b):
    return jnp.dot(a, b, preferred_element_type=F32)


def total(x):
    while x.ndim > 2:
        x = jnp.sum(x, axis=0)
    return jnp.sum(jnp.sum(x, axis=0, keepdims=True), axis=1, keepdims=True)


def add(a, b):
    return b if a is None else a if b is None else a + b


def scaled(c, factor):
    return [None if v is None else v * factor for v in c]


def plus(a, b):
    n = max(len(a), len(b))
    a, b = a + [None] * (n - len(a)), b + [None] * (n - len(b))
    return [add(v, w) for v, w in zip(a, b)]


def times(c):
    out = [None] * (len(c) + 1)
    for j, v in enumerate(c):
        if v is not None:
            out[j + 1] = add(out[j + 1], v)
            node = NODES[j % BLOCK]
            if node:
                out[j] = add(out[j], v * node)
    return out


def raised(c, count):
    out = [c]
    for k in range(count):
        node = NODES[k]
        out.append(plus(times(out[-1]), scaled(out[-1], -node) if node else [None]))
    return out


def inner(a, b, gram):
    out = None
    for i, v in enumerate(a):
        if v is not None:
            row = None
            for j, w in enumerate(b):
                if w is not None:
                    row = add(row, w * gram[min(i, j), max(i, j)])
            out = add(out, v * row)
    return out


def cg_steps(r, p, gram, image_of, last):
    x = [None]
    now = inner(r, r, gram)
    for step in range(BLOCK):
        image = image_of(p)
        alpha = now / inner(p, image, gram)
        x = plus(x, scaled(p, alpha))
        r = plus(r, scaled(image, -alpha))
        if last and step == BLOCK - 1:
            break
        new = inner(r, r, gram)
        p = plus(r, scaled(p, new / now))
        now = new
    return x, r, p


def combine(c, vectors):
    out = None
    for v, w in zip(c, vectors):
        if v is not None:
            out = [v * b for b in w] if out is None else [a + v * b for a, b in zip(out, w)]
    return out


def kernel(
    n_grp, n_sub, side, coef, damaged, owners, u_any, load_any, phase_any, soften_any, table_any,
    turn_any, inverse_any, field_ref, small_ref, tan_ref, u_ref, load_ref, kz, win, vs, ys,
    hx, hy, cells, seen_at, bc, chosen, table_ref, turn_ref, inverse_ref, hsend, hrecv, dsend,
    drecv, csend, crecv, bsend, brecv, tsend, trecv, fetch, gather,
):
    g = lax.axis_index("grp")
    s = lax.axis_index("sub")
    count = n_grp * n_sub
    me = g * n_sub + s
    rows_x, rows_y, rows_z = u_ref.shape
    planes = phase_any.shape[1]
    per = 128 // side
    wide = side * 8
    total_x, total_y = rows_x * n_grp, rows_y * n_sub
    win_x, win_y = kz.shape[0], kz.shape[1]
    pair = n_sub == 2
    own_y = pl.multiple_of(EDGE * s, EDGE) if pair else EDGE
    first_y = s * rows_y - own_y
    first_x = g * rows_x - DEPTH

    fetches = [
        pltpu.make_async_copy(a, b, fetch.at[i])
        for i, (a, b) in enumerate((
            (u_any, u_ref), (load_any, load_ref), (table_any, table_ref), (turn_any, turn_ref),
            (inverse_any, inverse_ref),
        ))
    ]
    barrier = pltpu.get_barrier_semaphore()
    fetches[0].start()
    own_cell = pl.ds(s * planes, planes)
    for i, ref in enumerate((phase_any, soften_any)):
        for j in range(side // per):
            pltpu.make_async_copy(
                ref.at[0, :, pl.ds(128 * j, 128)], cells.at[i, own_cell, j, :], gather.at[i]
            ).start()

    def greet(k, carry):
        other = lax.rem(me + k, count)
        pl.semaphore_signal(
            barrier, inc=1, device_id={"grp": other // n_sub, "sub": lax.rem(other, n_sub)},
            device_id_type=MESH,
        )
        return carry

    lax.fori_loop(1, count, greet, 0, unroll=8)
    for copy in fetches[1:]:
        copy.start()
    lane = lax.broadcasted_iota(jnp.int32, (1, 128), 1)
    line = lax.broadcasted_iota(jnp.int32, (1, rows_z), 1)

    def place(p):
        cell = damaged[p]
        rest = cell // rows_z
        return rest // total_y, lax.rem(rest, total_y), lax.rem(cell, rows_z)

    def row_of(values):
        out = jnp.zeros((1, 128), F32)
        for i, value in enumerate(values):
            out = out + jnp.where(lane == i, value, 0.0)
        return out

    def sample(row_x, row_y, z):
        at = lax.clamp(0, row_y, rows_y - 1)
        row = u_ref[lax.clamp(0, row_x, rows_x - 1), pl.ds(at, 1), :]
        inside = (row_x >= 0) & (row_x < rows_x) & (row_y >= 0) & (row_y < rows_y)
        keep = (line == z) & inside
        return jnp.sum(jnp.where(keep, row, 0.0), axis=1, keepdims=True)

    fetches[0].wait()
    qx, qy, qz = place(g)
    bx, by, bz = place(lax.max(g - 1, 0))
    qx, qy, by = qx - g * rows_x, qy - s * rows_y, by - s * rows_y
    bx = jnp.where(g > 0, bx + 1 - g * rows_x, -1)
    seen = row_of([
        sample(qx, qy, qz), sample(qx + 1, qy, qz), sample(qx, qy + 1, qz),
        sample(qx, qy, qz + 1), sample(bx, by, bz),
    ])
    for i, at in enumerate((0, rows_y - 1)):
        ys[i] = u_ref[:, at : at + 1, :]
    for i in range(2):
        block = cells.at[i, pl.ds(0, planes)]
        pltpu.make_async_copy(block, block, gather.at[i]).wait()

    pl.semaphore_wait(barrier, count - 1)

    g_up, g_down = lax.rem(g + 1, n_grp), lax.rem(g + n_grp - 1, n_grp)
    s_up, s_down = lax.rem(s + 1, n_sub), lax.rem(s + n_sub - 1, n_sub)

    def board(stage):
        return seen_at if stage == 0 else bc.at[stage - 1]

    def spread_start(stage, row):
        slots = board(stage)
        slots[me] = row

        upper = (2 * me) // count

        def send(k, carry):
            other = lax.rem(me + upper * k + (1 - upper) * (count - k), count)
            pltpu.make_async_remote_copy(
                src_ref=slots.at[me], dst_ref=slots.at[me],
                send_sem=bsend.at[stage], recv_sem=brecv.at[stage],
                device_id={"grp": other // n_sub, "sub": lax.rem(other, n_sub)}, device_id_type=MESH,
            ).start()
            return carry

        lax.fori_loop(1, count, send, 0, unroll=8)

    def spread_wait(stage):
        most = board(stage).at[pl.ds(0, count - 1)]
        pltpu.make_async_copy(most, most, brecv.at[stage]).wait()
        pltpu.make_async_copy(most, most, bsend.at[stage]).wait()

    def push(moves, send, recv):
        copies = []
        for i, (a, b, to_g, to_s) in enumerate(moves):
            copy = pltpu.make_async_remote_copy(
                src_ref=a, dst_ref=b, send_sem=send.at[i], recv_sem=recv.at[i],
                device_id={"grp": to_g, "sub": to_s}, device_id_type=MESH,
            )
            copy.start()
            copies.append(copy)
        return copies

    spread_start(0, seen)
    def cell_send(k, carry):
        to_s = lax.rem(s + k, n_sub)
        for i in range(2):
            pltpu.make_async_remote_copy(
                src_ref=cells.at[i, own_cell], dst_ref=cells.at[i, own_cell], send_sem=csend.at[i],
                recv_sem=crecv.at[i], device_id={"grp": g, "sub": to_s}, device_id_type=MESH,
            ).start()
        return carry

    halo_u = push(
        (
            (u_ref.at[rows_x - 1], hx.at[0], g_up, s), (u_ref.at[0], hx.at[1], g_down, s),
            (ys.at[1], hy.at[0], g, s_up), (ys.at[0], hy.at[1], g, s_down),
        ),
        hsend, hrecv,
    )
    lax.fori_loop(1, n_sub, cell_send, 0)

    def waves(at, base):
        return [jnp.cos(jnp.pi * (a + 1.0) * at / base) for a in range(4)]

    def twice(a):
        return jnp.concatenate([a] * (rows_z // 128), axis=1)

    def sheets_of(cos_y, cos_z):
        out = []
        for a in range(4):
            sheet = 0.0
            for b in range(4):
                row = coef[a + 4 * b] * cos_z[0] + coef[a + 4 * b + 16] * cos_z[1]
                sheet = sheet + row * cos_y[b]
            out.append(sheet)
        return out

    def logs(cos_x, sheets, i):
        return sum(twice(c[i : i + 1]) * sheet for c, sheet in zip(cos_x, sheets))

    at_z = line.astype(F32)
    tall = (win_x + 7) // 8 * 8
    along = lax.broadcasted_iota(jnp.int32, (tall, 128), 0)
    cos_x = waves((first_x + along).astype(F32) + 0.5, total_x)
    up = lax.broadcasted_iota(jnp.int32, (win_y, 128), 0)
    cos_y = [twice(c) for c in waves((first_y + up).astype(F32) + 0.5, total_y)]
    sheets = sheets_of(cos_y, waves(at_z + 0.5, rows_z))

    plane = (win_y, rows_z)
    y_at = lax.broadcasted_iota(jnp.int32, plane, 0)
    z_at = lax.broadcasted_iota(jnp.int32, plane, 1)
    within = None
    if not pair:
        within = ((first_y + y_at >= 0) & (first_y + y_at < total_y)).astype(F32)
    marks, spots, points = [], [], []
    for away in (-1, 0, 1):
        p = lax.clamp(0, g + away, n_grp - 1)
        x, y, z = place(p)
        valid = (g + away >= 0) & (g + away < n_grp)
        x = jnp.where(valid, x - first_x, -100)
        hit = (y_at == y - first_y) & (z_at == z)
        points.append(p)
        spots.append(x)
        marks.append(hit)
    rows_at = [jnp.where(hit, x, -100) for hit, x in zip(marks, spots)]
    marks = [jnp.where(hit, 1.0, 0.0) for hit in marks]

    def near(i):
        return 0 if i < DEPTH else 1 if i < DEPTH + rows_x else 2

    for i in range(win_x - 1):
        value = jnp.exp(0.4 * logs(cos_x, sheets, i))
        if i < DEPTH:
            value = value * (g > 0).astype(F32)
        if i >= DEPTH + rows_x:
            value = value * (g < n_grp - 1).astype(F32)
        if within is not None:
            value = value * within
        kz[i] = jnp.where(rows_at[near(i)] == i, 0.0, value)

    coarse = lax.broadcasted_iota(jnp.int32, (16, 128), 0).astype(F32)
    low = lax.broadcasted_iota(jnp.int32, (8, 128), 0).astype(F32)
    top_sheets = sheets_of([twice(c) for c in waves(low, 7)], waves(at_z, rows_z - 1))
    cos_t = waves(coarse, 15)
    top = logs(cos_t, top_sheets, 0)
    for i in range(1, 16):
        top = jnp.maximum(top, logs(cos_t, top_sheets, i))
    top = jnp.max(jnp.max(top, axis=0, keepdims=True), axis=1, keepdims=True)
    unit = 0.125 * jnp.exp(-0.4 * top)

    for copy in halo_u:
        copy.wait()
    fetches[1].wait()
    high_x = hx[1] * (g < n_grp - 1).astype(F32)
    below, above = hy[0] * (s > 0).astype(F32), hy[1] * (s < n_sub - 1).astype(F32)
    own_at_y = lax.broadcasted_iota(jnp.int32, (rows_y, rows_z), 0)
    own_at_z = lax.broadcasted_iota(jnp.int32, (rows_y, rows_z), 1)
    u = [u_ref[i] for i in range(rows_x)] + [high_x]
    before = kz[DEPTH - 1, pl.ds(own_y, rows_y), :] * (u[0] - hx[0])
    for i in range(rows_x):
        k = kz[DEPTH + i, pl.ds(own_y, rows_y), :]
        q0 = k * (u[i + 1] - u[i])
        q1 = k * (jnp.where(own_at_y == rows_y - 1, above[i], pltpu.roll(u[i], rows_y - 1, 0)) - u[i])
        q2 = k * (jnp.where(own_at_z == rows_z - 1, 0.0, pltpu.roll(u[i], rows_z - 1, 1)) - u[i])
        edge = kz[DEPTH + i, EDGE - 1 : EDGE, :] * (s > 0).astype(F32) * (u[i][0:1] - below[i])
        out = before - q0 + jnp.where(own_at_y == 0, edge, pltpu.roll(q1, 1, 0)) - q1
        out = out + jnp.where(own_at_z == 0, 0.0, pltpu.roll(q2, 1, 1)) - q2 + SHIFT * u[i]
        win[DEPTH + i, pl.ds(own_y, rows_y), :] = load_ref[i] - out
        before = q0

    send_up, send_down = pl.ds(rows_x, DEPTH), pl.ds(DEPTH, DEPTH)
    land_up, land_down = pl.ds(0, DEPTH), pl.ds(DEPTH + rows_x, DEPTH)
    middle = pl.ds(DEPTH, rows_x)
    sides = [(pl.ds(own_y, rows_y), pl.ds(own_y, rows_y), s)]
    if pair:
        there = pl.ds(pl.multiple_of(rows_y * s, EDGE), EDGE)
        sides.append((pl.ds(EDGE, EDGE), there, s_up))
    else:
        sides.append((pl.ds(rows_y, EDGE), pl.ds(0, EDGE), s_up))
        sides.append((pl.ds(EDGE, EDGE), pl.ds(EDGE + rows_y, EDGE), s_down))
    moves = []
    for source, target, to_s in sides:
        if to_s is not s:
            moves.append((win.at[middle, source], win.at[middle, target], g, to_s))
        moves.append((win.at[send_up, source], win.at[land_up, target], g_up, to_s))
        moves.append((win.at[send_down, source], win.at[land_down, target], g_down, to_s))
    halo_r = push(moves, dsend, drecv)

    for i in range(2):
        most = cells.at[i, pl.ds(0, planes * (n_sub - 1))]
        pltpu.make_async_copy(most, most, crecv.at[i]).wait()
        pltpu.make_async_copy(most, most, csend.at[i]).wait()
    for copy in fetches[2:]:
        copy.wait()
    spread_wait(0)

    def entry_of(row, i):
        return jnp.sum(jnp.where(lane == i, row, 0.0), axis=1, keepdims=True)

    def strain(q):
        after = lax.min(q + 1, n_grp - 1)
        row = sum(seen_at[q * n_sub + i] for i in range(n_sub))
        more = sum(seen_at[after * n_sub + i] for i in range(n_sub))
        more = jnp.where(q < n_grp - 1, more, 0.0)
        row = row + jnp.where(lane == 1, pltpu.roll(more, 125, 1), 0.0)
        values = [entry_of(row, i) for i in range(4)]
        return [v - values[0] for v in values[1:]]

    mine = sum(jnp.where(owners[q] == g, q, 0) for q in range(n_grp))
    mine = lax.min(mine, n_grp - 1)
    strength = sum(v * v for v in strain(mine))
    cond = cells[0] / (1.0 + cells[1] * strength)
    turned = [cond - K0]
    turned += [pltpu.roll(turned[0], i * side, 2) for i in range(1, per)]
    cube = (side, side, 128)
    cell_lane = lax.broadcasted_iota(jnp.int32, (1, 8, 128), 2)
    group = cell_lane // side
    in_group = lax.rem(cell_lane, side)
    parts = []
    for t in range(per):
        part = turned[(0 - t) % per]
        for j in range(1, per):
            part = jnp.where(group == j, turned[(j - t) % per], part)
        parts.append(part)
    shift_k = parts

    def ahead(v, axis):
        if axis == 0:
            return [jnp.concatenate([a[1:], a[:1]], 0) for a in v]
        if axis == 1:
            return v[1:] + [pltpu.roll(v[0], 7, 1)]
        return [
            jnp.where(in_group == side - 1, pltpu.roll(a, side - 1, 2), pltpu.roll(a, 127, 2))
            for a in v
        ]

    def behind(v, axis):
        if axis == 0:
            return [jnp.concatenate([a[-1:], a[:-1]], 0) for a in v]
        if axis == 1:
            return [pltpu.roll(v[-1], 1, 1)] + v[:-1]
        return [
            jnp.where(in_group == 0, pltpu.roll(a, 129 - side, 2), pltpu.roll(a, 1, 2)) for a in v
        ]

    def right(v):
        high, low = split(v)
        both = mm(jnp.concatenate([high, low], axis=1), turn_ref[...])
        return both[:, :128] + both[:, 128:]

    def left(t, v):
        high, low = split(v)
        both = mm(table_ref[t], high)
        return both[:wide] + both[wide:] + mm(table_ref[t, :wide], low)

    def halves(a, b, t):
        out = left(t, jnp.concatenate([a, b], axis=1))
        return out[:, :128], out[:, 128:]

    def along_z(v):
        return [right(a.reshape(wide, 128)).reshape(side, 8, 128) for a in v]

    def along_x(v):
        out = []
        for i in range(0, per, 2):
            for a in halves(v[i].reshape(wide, 128), v[i + 1].reshape(wide, 128), 1):
                out.append(a.reshape(side, 8, 128))
        return out

    def along_y(v):
        out = [[] for _ in range(per)]
        for i in range(0, side, 16):
            blocks = [
                jnp.concatenate([a[j : j + 8] for a in v], axis=1).reshape(wide, 128)
                for j in (i, i + 8)
            ]
            for block in halves(blocks[0], blocks[1], 0):
                block = block.reshape(8, side, 128)
                for t in range(per):
                    out[t].append(block[:, 8 * t : 8 * t + 8])
        return [jnp.concatenate(a, axis=0) for a in out]

    def solve(div):
        spectrum = along_x(along_y(along_z(div)))
        spectrum = [a * inverse_ref[:, 8 * t : 8 * t + 8] for t, a in enumerate(spectrum)]
        return along_z(along_y(along_x(spectrum)))

    def div_of(phi):
        out = [0.0] * per
        for axis in range(3):
            tau = [k * (a - b) for k, a, b in zip(shift_k, ahead(phi, axis), phi)]
            out = [o + a - b for o, a, b in zip(out, tau, behind(tau, axis))]
        return out

    backs = [behind(shift_k, axis) for axis in range(3)]
    div1 = []
    for t in range(per):
        back = jnp.where(group == 0, backs[0][t], shift_k[t])
        back = jnp.where(group == 1, backs[1][t], back)
        div1.append(shift_k[t] - jnp.where(group == 2, backs[2][t], back))
    phi1 = solve(div1)
    div2 = div_of(phi1)
    phi2 = solve(div2)
    div3 = div_of(phi2)
    first = [a + b for a, b in zip(div1, div2)]
    second = [a + b for a, b in zip(div2, div3)]
    volume = float(side**3)
    mean = total(cond) / volume
    entry = {}
    for turn in range(3):
        sums = 0.0
        for t in range(per):
            a = phi1[t] if turn == 0 else pltpu.roll(phi1[t], turn * side, 2)
            b = phi2[t] if turn == 0 else pltpu.roll(phi2[t], turn * side, 2)
            sums = sums + jnp.sum(a * first[t] + b * second[t], axis=0)
        sums = jnp.sum(sums, axis=0, keepdims=True)
        for j in range(turn, 3):
            value = -jnp.sum(
                jnp.where(lane // side == j, sums, 0.0), axis=1, keepdims=True
            ) / volume
            entry[j - turn, j] = entry[j, j - turn] = value + mean if turn == 0 else value
    row = jnp.zeros((1, 128), F32)
    for i in range(3):
        for j in range(3):
            row = row + jnp.where(lane == 3 * i + j, entry[i, j], 0.0)
    tan_ref[g] = row

    upper_g = (2 * g) // n_grp

    def tangent_send(k, carry):
        to_g = lax.rem(g + upper_g * k + (1 - upper_g) * (n_grp - k), n_grp)
        pltpu.make_async_remote_copy(
            src_ref=tan_ref.at[g], dst_ref=tan_ref.at[g], send_sem=tsend, recv_sem=trecv,
            device_id={"grp": to_g, "sub": s}, device_id_type=MESH,
        ).start()
        return carry

    lax.fori_loop(1, n_grp, tangent_send, 0, unroll=5)

    strains = [strain(p) for p in points]
    small = SHIFT * unit
    for i in range(win_x - 1):
        kz[i] = kz[i] * unit
    for copy in halo_r:
        copy.wait()

    most = tan_ref.at[pl.ds(0, n_grp - 1)]
    pltpu.make_async_copy(most, most, trecv).wait()
    pltpu.make_async_copy(most, most, tsend).wait()

    def tensor(p):
        row = tan_ref[owners[p]]
        return {(i, j): entry_of(row, 3 * i + j) for i in range(3) for j in range(i, 3)}

    tensors = [tensor(p) for p in points]

    def rows_times(t, d):
        return [
            sum(t[min(i, j), max(i, j)] * d[j] for j in range(3)) for i in range(3)
        ]

    def next_y(v):
        return jnp.where(y_at == win_y - 1, 0.0, pltpu.roll(v, win_y - 1, 0))

    def next_z(v):
        return jnp.where(z_at == rows_z - 1, 0.0, pltpu.roll(v, rows_z - 1, 1))

    def last_y(v):
        return jnp.where(y_at == 0, 0.0, pltpu.roll(v, 1, 0))

    def last_z(v):
        return jnp.where(z_at == 0, 0.0, pltpu.roll(v, 1, 1))

    def stencil(e):
        return last_y(e[1]) + last_z(e[2]) - e[0] - e[1] - e[2]

    fixes = []
    for t, d, mark in zip(tensors, strains, marks):
        e = [v * mark for v in rows_times(t, d)]
        fixes.append((e[0], stencil(e)))

    wide_at = [jnp.broadcast_to(x, plane) for x in spots]

    def fix(out, i, fixes, first):
        x, center = fixes[near(i)]
        out = out + jnp.where(wide_at[near(i)] == i, center, 0.0)
        if i > first:
            x, center = fixes[near(i - 1)]
            out = out + jnp.where(wide_at[near(i - 1)] == i - 1, x, 0.0)
        return out

    for i in range(win_x):
        value = win[i]
        if i < DEPTH:
            value = value * (g > 0).astype(F32)
        if i >= DEPTH + rows_x:
            value = value * (g < n_grp - 1).astype(F32)
        if within is not None:
            value = value * within
        out = fix(jnp.zeros(plane, F32), i, fixes, 0)
        if i == DEPTH + rows_x:
            out = out * (g < n_grp - 1).astype(F32)
        vs[0, i] = value - out

    unit_tensors = [
        {k: jnp.broadcast_to(v * unit, (8, 128)) for k, v in t.items()} for t in tensors
    ]

    sub_at = lax.broadcasted_iota(jnp.int32, (8, 128), 0)
    lane_at = lax.broadcasted_iota(jnp.int32, (8, 128), 1)
    tiles_y, tiles_z = win_y // 8, rows_z // 128
    cells_at = [(a, b) for a in range(tiles_y) for b in range(tiles_z)]

    def tiles_of(ref, *at):
        return {
            (a, b): ref[(*at, pl.ds(8 * a, 8), pl.ds(128 * b, 128))] for a, b in cells_at
        }

    def cut(v):
        return {(a, b): v[8 * a : 8 * a + 8, 128 * b : 128 * b + 128] for a, b in cells_at}

    def moved(v, axis, by):
        size = (8, 128)[axis]
        rolled = {key: pltpu.roll(w, by % size, axis) for key, w in v.items()}
        edge = (sub_at, lane_at)[axis] == (size - 1 if by < 0 else 0)
        out = {}
        for a, b in v:
            other = (a - by, b) if axis == 0 else (a, b - by)
            out[a, b] = jnp.where(edge, rolled.get(other, 0.0), rolled[a, b])
        return out

    spot_marks = [cut(mark) for mark in marks]
    spot_at = [jnp.broadcast_to(x, (8, 128)) for x in spots]
    hits = {(near(i), i): spot_at[near(i)] == i for i in range(win_x)}

    def advance(k):
        first, end = k, win_x - k
        node = NODES[k % BLOCK]
        keep = jnp.broadcast_to(small - node if node else small, (8, 128))
        v = tiles_of(vs, k, first)
        before = None
        for i in range(first, end - 1):
            after = tiles_of(vs, k, i + 1)
            weight = tiles_of(kz, i)
            n = near(i)
            up_y, up_z = moved(v, 0, -1), moved(v, 1, -1)
            q = [{}, {}, {}]
            for c in cells_at:
                mark = jnp.where(hits[n, i], spot_marks[n][c], 0.0)
                d = after[c] - v[c], up_y[c] - v[c], up_z[c] - v[c]
                extra = rows_times(unit_tensors[n], [mark * value for value in d])
                for j in range(3):
                    q[j][c] = weight[c] * d[j] + extra[j]
            if before is not None:
                low_y, low_z = moved(q[1], 0, 1), moved(q[2], 1, 1)
                for a, b in cells_at:
                    c = a, b
                    out = (before[c] - q[0][c]) + (low_y[c] - q[1][c])
                    out = out + ((low_z[c] - q[2][c]) + keep * v[c])
                    if i == DEPTH + rows_x:
                        out = out * (g < n_grp - 1).astype(F32)
                    if within is not None:
                        out = out * within[8 * a : 8 * a + 8, 128 * b : 128 * b + 128]
                    vs[k + 1, i, pl.ds(8 * a, 8), pl.ds(128 * b, 128)] = out
            before, v = q[0], after

    def own_of(k):
        return [vs[k, DEPTH + i, pl.ds(own_y, rows_y), :] for i in range(rows_x)]

    def dot(a, b):
        out = None
        for v, w in zip(a, b):
            out = add(out, v * w)
        parts = [
            out[i : i + 8, j : j + 128] for i in range(0, rows_y, 8) for j in range(0, rows_z, 128)
        ]
        return jnp.sum(sum(parts), axis=0, keepdims=True)

    def packed_row(parts, start=0):
        n = len(parts)
        column = jnp.sum(jnp.concatenate(parts, axis=0), axis=1, keepdims=True)
        down = lax.broadcasted_iota(jnp.int32, (n, 128), 0)
        across = lax.broadcasted_iota(jnp.int32, (n, 128), 1)
        return jnp.sum(jnp.where(across == down + start, column, 0.0), axis=0, keepdims=True)

    for k in range(BLOCK):
        advance(k)
    v = [own_of(k) for k in range(BLOCK + 1)]
    pairs = [(i, j) for i in range(BLOCK + 1) for j in range(i, BLOCK + 1)]
    spread_start(1, packed_row([dot(v[i], v[j]) for i, j in pairs]))
    for k in range(BLOCK, CG_ITERS):
        advance(k)
    for q in range(n_grp):
        chosen[q] = tan_ref[owners[q]]
    v += [own_of(k) for k in range(BLOCK + 1, CG_ITERS + 1)]

    has_point = (qy >= 0) & (qy < rows_y)
    here_x = lax.clamp(DEPTH, spots[1], DEPTH + rows_x - 1)
    here_y = lax.clamp(0, qy + own_y, win_y - 1)
    next_row = lax.clamp(0, qy + own_y + 1, win_y - 1)
    at_top = qy + own_y + 1 > win_y - 1
    here = (line == qz) & has_point
    slopes = []
    for k in range(CG_ITERS):
        base = vs[k, here_x, pl.ds(here_y, 1), :]
        side_x = vs[k, here_x + 1, pl.ds(here_y, 1), :]
        side_y = jnp.where(at_top, 0.0, vs[k, here_x, pl.ds(next_row, 1), :])
        side_z = jnp.where(line == rows_z - 1, 0.0, pltpu.roll(base, rows_z - 1, 1))
        for other in (side_x, side_y, side_z):
            value = jnp.where(here, other - base, 0.0)
            slopes.append(sum(value[:, j : j + 128] for j in range(0, rows_z, 128)))
    slope_at = 64
    slope_row = packed_row(slopes, slope_at)

    spread_wait(1)
    sums = jnp.sum(bc[0], axis=0)
    gram = {key: entry_of(sums, n) for n, key in enumerate(pairs)}
    one = [jnp.ones((1, 1), F32)]
    x_c, r_c, p_c = cg_steps(one, one, gram, times, False)
    r_powers, p_powers = raised(r_c, BLOCK - 1), raised(p_c, BLOCK)
    powers = r_powers + p_powers
    basis = [combine(c, v) for c in powers]
    width = BLOCK + BLOCK + 1
    pairs = [(i, j) for i in range(width) for j in range(i, width)]
    pairs = [key for key in pairs if key not in ((BLOCK - 1,) * 2, (BLOCK - 1, width - 1), (width - 1,) * 2)]
    spread_start(2, packed_row([dot(basis[i], basis[j]) for i, j in pairs]) + slope_row)
    x = combine(x_c, v)

    def image_of(c):
        c = c + [None] * (width - len(c))
        a, b = times(c[: BLOCK - 1]), times(c[BLOCK : width - 1])
        return a + [None] * (BLOCK - len(a)) + b

    spread_wait(2)
    got = bc[1]
    sums = jnp.sum(got, axis=0)
    gram = {key: entry_of(sums, n) for n, key in enumerate(pairs)}
    start = [None] * BLOCK + one
    x2_c, r2_c, _ = cg_steps(one, start, gram, image_of, True)
    x = combine([one[0]] + x2_c, [x] + basis)
    r = combine(r2_c, basis)
    for i in range(rows_x):
        field_ref[0, i] = x[i] * unit
        field_ref[1, i] = r[i]
    whole = x_c
    for c, power in zip(x2_c, powers):
        if c is not None:
            whole = plus(whole, scaled(power, c))
    slope = jnp.sum(got.reshape(n_grp, n_sub, 1, 128), axis=1)
    spot = lax.broadcasted_iota(jnp.int32, slope.shape, 2)
    weights = jnp.zeros((1, 128), F32)
    for k in range(CG_ITERS):
        inside = (lane >= slope_at + 3 * k) & (lane < slope_at + 3 * k + 3)
        weights = weights + jnp.where(inside, whole[k] * unit, 0.0)
    slope = slope * weights[None]
    product = 0.0
    for j in range(3):
        inside = (spot >= slope_at) & (spot < slope_at + 3 * CG_ITERS)
        inside = inside & (lax.rem(spot - slope_at + 3, 3) == j)
        part = jnp.sum(jnp.where(inside, slope, 0.0), axis=2, keepdims=True)
        product = product + jnp.where((lax.rem(spot, 3) == j) & (spot < 9), chosen[...], 0.0) * part
    out = jnp.zeros_like(slope)
    for i in range(3):
        part = jnp.sum(jnp.where(spot // 3 == i, product, 0.0), axis=2, keepdims=True)
        out = out + jnp.where(spot == 9 + i, part, 0.0)
    for q in range(n_grp):
        small_ref[q : q + 1] = jnp.where(lane < 9, tan_ref[q], out[q])


def tables(side):
    index = np.arange(side)
    per = 128 // side
    place = np.arange(side).reshape(side // per, per).T.reshape(-1)
    angle = 2.0 * np.pi * (np.outer(index, index) % side) / side
    hartley = (np.cos(angle) + np.sin(angle)) / np.sqrt(side)

    def halves(a):
        a = a.astype(np.float32)
        high = a.astype(jnp.bfloat16)
        return high, (a - high.astype(np.float32)).astype(jnp.bfloat16)

    kinds = np.kron(np.eye(8), hartley[place][:, place]), np.kron(hartley, np.eye(8))
    table = np.stack([np.concatenate(halves(a), axis=0) for a in kinds])
    high, low = halves(np.kron(np.eye(per), hartley))
    turn = np.block([[high, low], [high, np.zeros_like(low)]])
    line = 4.0 * np.sin(np.pi * index / side) ** 2
    lam = line[:, None, None] + line[None, place, None] + line[None, None, :]
    lam[0, 0, 0] = 1.0
    inverse = 1.0 / (K0 * lam)
    inverse[0, 0, 0] = 0.0
    return table, turn, np.tile(inverse.astype(np.float32), (1, 1, per))


def body(displacement, load, kl_coef, damaged, owner, phase, soften):
    n_grp, n_sub = lax.axis_size("grp"), lax.axis_size("sub")
    count = n_grp * n_sub
    rows_x, rows_y, rows_z = displacement.shape
    planes = phase.shape[1]
    side = math.isqrt(phase.shape[2])
    table, turn, inverse = tables(side)
    points = owner.shape[0]
    win_x = rows_x + 2 * DEPTH
    win_y = rows_y + (EDGE if n_sub == 2 else 2 * EDGE)
    moves = 5 if n_sub == 2 else 8
    vmem = pl.BlockSpec(memory_space=pltpu.VMEM)
    smem = pl.BlockSpec(memory_space=pltpu.SMEM)
    fields, small = pl.pallas_call(
        functools.partial(kernel, n_grp, n_sub, side),
        out_shape=[
            jax.ShapeDtypeStruct((2, *displacement.shape), F32),
            jax.ShapeDtypeStruct((points, 128), F32),
        ],
        in_specs=[smem] * 3 + [pl.BlockSpec(memory_space=pl.ANY)] * 7,
        out_specs=[vmem] * 2,
        scratch_shapes=[
            pltpu.VMEM((n_grp, 1, 128), F32),
            pltpu.VMEM(displacement.shape, F32),
            pltpu.VMEM(displacement.shape, F32),
            pltpu.VMEM((win_x, win_y, rows_z), F32),
            pltpu.VMEM((win_x, win_y, rows_z), F32),
            pltpu.VMEM((CG_ITERS + 1, win_x, win_y, rows_z), F32),
            pltpu.VMEM((2, rows_x, 1, rows_z), F32),
            pltpu.VMEM((2, rows_y, rows_z), F32),
            pltpu.VMEM((2, rows_x, 1, rows_z), F32),
            pltpu.VMEM((2, side, side * side // 128, 128), F32),
            pltpu.VMEM((count, 1, 128), F32),
            pltpu.VMEM((2, count, 1, 128), F32),
            pltpu.VMEM((points, 1, 128), F32),
            pltpu.VMEM(table.shape, BF16),
            pltpu.VMEM(turn.shape, BF16),
            pltpu.VMEM(inverse.shape, F32),
            pltpu.SemaphoreType.DMA((4,)),
            pltpu.SemaphoreType.DMA((4,)),
            pltpu.SemaphoreType.DMA((moves,)),
            pltpu.SemaphoreType.DMA((moves,)),
            pltpu.SemaphoreType.DMA((2,)),
            pltpu.SemaphoreType.DMA((2,)),
            pltpu.SemaphoreType.DMA((3,)),
            pltpu.SemaphoreType.DMA((3,)),
            pltpu.SemaphoreType.DMA,
            pltpu.SemaphoreType.DMA,
            pltpu.SemaphoreType.DMA((5,)),
            pltpu.SemaphoreType.DMA((2,)),
        ],
        compiler_params=pltpu.CompilerParams(collective_id=0, has_side_effects=True),
    )(kl_coef, damaged, owner, displacement, load, phase, soften, jnp.asarray(table),
      jnp.asarray(turn), jnp.asarray(inverse))
    return fields[0], fields[1], small[:, :9], small[:, 9:12]


def solution(mesh):
    return jax.shard_map(
        body,
        mesh=mesh,
        in_specs=(
            P("grp", "sub", None), P("grp", "sub", None), P(), P(), P(),
            P("grp", "sub", None), P("grp", "sub", None),
        ),
        out_specs=(P("grp", "sub", None), P("grp", "sub", None), P(), P()),
        check_vma=False,
    )
```

```python
import functools
import math

import jax
import jax.numpy as jnp
import numpy as np
from jax import lax
from jax.experimental import pallas as pl
from jax.experimental.pallas import tpu as pltpu
from jax.sharding import PartitionSpec as P

CG_ITERS = 6
BLOCK = CG_ITERS // 2
NODES = (0.0, 0.7, 0.25)
DEPTH = CG_ITERS
EDGE = 8
K0 = 6.0
SHIFT = 0.002
MESH = pl.DeviceIdType.MESH
F32 = jnp.float32
BF16 = jnp.bfloat16


def split(x):
    high = x.astype(BF16)
    return high, (x - high.astype(F32)).astype(BF16)


def mm(a, b):
    return jnp.dot(a, b, preferred_element_type=F32)


def total(x):
    while x.ndim > 2:
        x = jnp.sum(x, axis=0)
    return jnp.sum(jnp.sum(x, axis=0, keepdims=True), axis=1, keepdims=True)


def add(a, b):
    return b if a is None else a if b is None else a + b


def scaled(c, factor):
    return [None if v is None else v * factor for v in c]


def plus(a, b):
    n = max(len(a), len(b))
    a, b = a + [None] * (n - len(a)), b + [None] * (n - len(b))
    return [add(v, w) for v, w in zip(a, b)]


def times(c):
    out = [None] * (len(c) + 1)
    for j, v in enumerate(c):
        if v is not None:
            out[j + 1] = add(out[j + 1], v)
            node = NODES[j % BLOCK]
            if node:
                out[j] = add(out[j], v * node)
    return out


def raised(c, count):
    out = [c]
    for k in range(count):
        node = NODES[k]
        out.append(plus(times(out[-1]), scaled(out[-1], -node) if node else [None]))
    return out


def inner(a, b, gram):
    out = None
    for i, v in enumerate(a):
        if v is not None:
            row = None
            for j, w in enumerate(b):
                if w is not None:
                    row = add(row, w * gram[min(i, j), max(i, j)])
            out = add(out, v * row)
    return out


def cg_steps(r, p, gram, image_of, last):
    x = [None]
    now = inner(r, r, gram)
    for step in range(BLOCK):
        image = image_of(p)
        alpha = now / inner(p, image, gram)
        x = plus(x, scaled(p, alpha))
        r = plus(r, scaled(image, -alpha))
        if last and step == BLOCK - 1:
            break
        new = inner(r, r, gram)
        p = plus(r, scaled(p, new / now))
        now = new
    return x, r, p


def combine(c, vectors):
    out = None
    for v, w in zip(c, vectors):
        if v is not None:
            out = [v * b for b in w] if out is None else [a + v * b for a, b in zip(out, w)]
    return out


def kernel(
    n_grp, n_sub, side, coef, damaged, owners, u_any, load_any, phase_any, soften_any, table_any,
    turn_any, inverse_any, field_ref, small_ref, tan_ref, u_ref, load_ref, kz, win, vs, ys,
    hx, hy, cells, seen_at, bc, chosen, table_ref, turn_ref, inverse_ref, hsend, hrecv, dsend,
    drecv, csend, crecv, bsend, brecv, tsend, trecv, fetch, gather,
):
    g = lax.axis_index("grp")
    s = lax.axis_index("sub")
    count = n_grp * n_sub
    me = g * n_sub + s
    rows_x, rows_y, rows_z = u_ref.shape
    planes = phase_any.shape[1]
    per = 128 // side
    wide = side * 8
    total_x, total_y = rows_x * n_grp, rows_y * n_sub
    win_x, win_y = kz.shape[0], kz.shape[1]
    pair = n_sub == 2
    own_y = pl.multiple_of(EDGE * s, EDGE) if pair else EDGE
    first_y = s * rows_y - own_y
    first_x = g * rows_x - DEPTH

    fetches = [
        pltpu.make_async_copy(a, b, fetch.at[i])
        for i, (a, b) in enumerate((
            (u_any, u_ref), (load_any, load_ref), (table_any, table_ref), (turn_any, turn_ref),
            (inverse_any, inverse_ref),
        ))
    ]
    barrier = pltpu.get_barrier_semaphore()
    fetches[0].start()
    own_cell = pl.ds(s * planes, planes)
    for i, ref in enumerate((phase_any, soften_any)):
        for j in range(side // per):
            pltpu.make_async_copy(
                ref.at[0, :, pl.ds(128 * j, 128)], cells.at[i, own_cell, j, :], gather.at[i]
            ).start()

    def greet(k, carry):
        other = lax.rem(me + k, count)
        pl.semaphore_signal(
            barrier, inc=1, device_id={"grp": other // n_sub, "sub": lax.rem(other, n_sub)},
            device_id_type=MESH,
        )
        return carry

    lax.fori_loop(1, count, greet, 0, unroll=31)
    for copy in fetches[1:]:
        copy.start()
    lane = lax.broadcasted_iota(jnp.int32, (1, 128), 1)
    line = lax.broadcasted_iota(jnp.int32, (1, rows_z), 1)

    def place(p):
        cell = damaged[p]
        rest = cell // rows_z
        return rest // total_y, lax.rem(rest, total_y), lax.rem(cell, rows_z)

    def row_of(values):
        out = jnp.zeros((1, 128), F32)
        for i, value in enumerate(values):
            out = out + jnp.where(lane == i, value, 0.0)
        return out

    def sample(row_x, row_y, z):
        at = lax.clamp(0, row_y, rows_y - 1)
        row = u_ref[lax.clamp(0, row_x, rows_x - 1), pl.ds(at, 1), :]
        inside = (row_x >= 0) & (row_x < rows_x) & (row_y >= 0) & (row_y < rows_y)
        keep = (line == z) & inside
        return jnp.sum(jnp.where(keep, row, 0.0), axis=1, keepdims=True)

    fetches[0].wait()
    qx, qy, qz = place(g)
    bx, by, bz = place(lax.max(g - 1, 0))
    qx, qy, by = qx - g * rows_x, qy - s * rows_y, by - s * rows_y
    bx = jnp.where(g > 0, bx + 1 - g * rows_x, -1)
    seen = row_of([
        sample(qx, qy, qz), sample(qx + 1, qy, qz), sample(qx, qy + 1, qz),
        sample(qx, qy, qz + 1), sample(bx, by, bz),
    ])
    for i, at in enumerate((0, rows_y - 1)):
        ys[i] = u_ref[:, at : at + 1, :]
    for i in range(2):
        block = cells.at[i, pl.ds(0, planes)]
        pltpu.make_async_copy(block, block, gather.at[i]).wait()

    pl.semaphore_wait(barrier, count - 1)

    g_up, g_down = lax.rem(g + 1, n_grp), lax.rem(g + n_grp - 1, n_grp)
    s_up, s_down = lax.rem(s + 1, n_sub), lax.rem(s + n_sub - 1, n_sub)

    def board(stage):
        return seen_at if stage == 0 else bc.at[stage - 1]

    def spread_start(stage, row):
        slots = board(stage)
        slots[me] = row

        upper = (2 * me) // count

        def send(k, carry):
            other = lax.rem(me + upper * k + (1 - upper) * (count - k), count)
            pltpu.make_async_remote_copy(
                src_ref=slots.at[me], dst_ref=slots.at[me],
                send_sem=bsend.at[stage], recv_sem=brecv.at[stage],
                device_id={"grp": other // n_sub, "sub": lax.rem(other, n_sub)}, device_id_type=MESH,
            ).start()
            return carry

        lax.fori_loop(1, count, send, 0, unroll=31)

    def spread_wait(stage):
        most = board(stage).at[pl.ds(0, count - 1)]
        pltpu.make_async_copy(most, most, brecv.at[stage]).wait()
        pltpu.make_async_copy(most, most, bsend.at[stage]).wait()

    def push(moves, send, recv):
        copies = []
        for i, (a, b, to_g, to_s) in enumerate(moves):
            copy = pltpu.make_async_remote_copy(
                src_ref=a, dst_ref=b, send_sem=send.at[i], recv_sem=recv.at[i],
                device_id={"grp": to_g, "sub": to_s}, device_id_type=MESH,
            )
            copy.start()
            copies.append(copy)
        return copies

    spread_start(0, seen)
    def cell_send(k, carry):
        to_s = lax.rem(s + k, n_sub)
        for i in range(2):
            pltpu.make_async_remote_copy(
                src_ref=cells.at[i, own_cell], dst_ref=cells.at[i, own_cell], send_sem=csend.at[i],
                recv_sem=crecv.at[i], device_id={"grp": g, "sub": to_s}, device_id_type=MESH,
            ).start()
        return carry

    halo_u = push(
        (
            (u_ref.at[rows_x - 1], hx.at[0], g_up, s), (u_ref.at[0], hx.at[1], g_down, s),
            (ys.at[1], hy.at[0], g, s_up), (ys.at[0], hy.at[1], g, s_down),
        ),
        hsend, hrecv,
    )
    lax.fori_loop(1, n_sub, cell_send, 0)

    def waves(at, base):
        return [jnp.cos(jnp.pi * (a + 1.0) * at / base) for a in range(4)]

    def twice(a):
        return jnp.concatenate([a] * (rows_z // 128), axis=1)

    def sheets_of(cos_y, cos_z):
        out = []
        for a in range(4):
            sheet = 0.0
            for b in range(4):
                row = coef[a + 4 * b] * cos_z[0] + coef[a + 4 * b + 16] * cos_z[1]
                sheet = sheet + row * cos_y[b]
            out.append(sheet)
        return out

    def logs(cos_x, sheets, i):
        return sum(twice(c[i : i + 1]) * sheet for c, sheet in zip(cos_x, sheets))

    at_z = line.astype(F32)
    tall = (win_x + 7) // 8 * 8
    along = lax.broadcasted_iota(jnp.int32, (tall, 128), 0)
    cos_x = waves((first_x + along).astype(F32) + 0.5, total_x)
    up = lax.broadcasted_iota(jnp.int32, (win_y, 128), 0)
    cos_y = [twice(c) for c in waves((first_y + up).astype(F32) + 0.5, total_y)]
    sheets = sheets_of(cos_y, waves(at_z + 0.5, rows_z))

    plane = (win_y, rows_z)
    y_at = lax.broadcasted_iota(jnp.int32, plane, 0)
    z_at = lax.broadcasted_iota(jnp.int32, plane, 1)
    within = None
    if not pair:
        within = ((first_y + y_at >= 0) & (first_y + y_at < total_y)).astype(F32)
    marks, spots, points = [], [], []
    for away in (-1, 0, 1):
        p = lax.clamp(0, g + away, n_grp - 1)
        x, y, z = place(p)
        valid = (g + away >= 0) & (g + away < n_grp)
        x = jnp.where(valid, x - first_x, -100)
        hit = (y_at == y - first_y) & (z_at == z)
        points.append(p)
        spots.append(x)
        marks.append(hit)
    rows_at = [jnp.where(hit, x, -100) for hit, x in zip(marks, spots)]
    marks = [jnp.where(hit, 1.0, 0.0) for hit in marks]

    def near(i):
        return 0 if i < DEPTH else 1 if i < DEPTH + rows_x else 2

    for i in range(win_x - 1):
        value = jnp.exp(0.4 * logs(cos_x, sheets, i))
        if i < DEPTH:
            value = value * (g > 0).astype(F32)
        if i >= DEPTH + rows_x:
            value = value * (g < n_grp - 1).astype(F32)
        if within is not None:
            value = value * within
        kz[i] = jnp.where(rows_at[near(i)] == i, 0.0, value)

    coarse = lax.broadcasted_iota(jnp.int32, (16, 128), 0).astype(F32)
    low = lax.broadcasted_iota(jnp.int32, (8, 128), 0).astype(F32)
    top_sheets = sheets_of([twice(c) for c in waves(low, 7)], waves(at_z, rows_z - 1))
    cos_t = waves(coarse, 15)
    top = logs(cos_t, top_sheets, 0)
    for i in range(1, 16):
        top = jnp.maximum(top, logs(cos_t, top_sheets, i))
    top = jnp.max(jnp.max(top, axis=0, keepdims=True), axis=1, keepdims=True)
    unit = 0.125 * jnp.exp(-0.4 * top)

    for copy in halo_u:
        copy.wait()
    fetches[1].wait()
    high_x = hx[1] * (g < n_grp - 1).astype(F32)
    below, above = hy[0] * (s > 0).astype(F32), hy[1] * (s < n_sub - 1).astype(F32)
    own_at_y = lax.broadcasted_iota(jnp.int32, (rows_y, rows_z), 0)
    own_at_z = lax.broadcasted_iota(jnp.int32, (rows_y, rows_z), 1)
    u = [u_ref[i] for i in range(rows_x)] + [high_x]
    before = kz[DEPTH - 1, pl.ds(own_y, rows_y), :] * (u[0] - hx[0])
    for i in range(rows_x):
        k = kz[DEPTH + i, pl.ds(own_y, rows_y), :]
        q0 = k * (u[i + 1] - u[i])
        q1 = k * (jnp.where(own_at_y == rows_y - 1, above[i], pltpu.roll(u[i], rows_y - 1, 0)) - u[i])
        q2 = k * (jnp.where(own_at_z == rows_z - 1, 0.0, pltpu.roll(u[i], rows_z - 1, 1)) - u[i])
        edge = kz[DEPTH + i, EDGE - 1 : EDGE, :] * (s > 0).astype(F32) * (u[i][0:1] - below[i])
        out = before - q0 + jnp.where(own_at_y == 0, edge, pltpu.roll(q1, 1, 0)) - q1
        out = out + jnp.where(own_at_z == 0, 0.0, pltpu.roll(q2, 1, 1)) - q2 + SHIFT * u[i]
        win[DEPTH + i, pl.ds(own_y, rows_y), :] = load_ref[i] - out
        before = q0

    send_up, send_down = pl.ds(rows_x, DEPTH), pl.ds(DEPTH, DEPTH)
    land_up, land_down = pl.ds(0, DEPTH), pl.ds(DEPTH + rows_x, DEPTH)
    middle = pl.ds(DEPTH, rows_x)
    sides = [(pl.ds(own_y, rows_y), pl.ds(own_y, rows_y), s)]
    if pair:
        there = pl.ds(pl.multiple_of(rows_y * s, EDGE), EDGE)
        sides.append((pl.ds(EDGE, EDGE), there, s_up))
    else:
        sides.append((pl.ds(rows_y, EDGE), pl.ds(0, EDGE), s_up))
        sides.append((pl.ds(EDGE, EDGE), pl.ds(EDGE + rows_y, EDGE), s_down))
    moves = []
    for source, target, to_s in sides:
        if to_s is not s:
            moves.append((win.at[middle, source], win.at[middle, target], g, to_s))
        moves.append((win.at[send_up, source], win.at[land_up, target], g_up, to_s))
        moves.append((win.at[send_down, source], win.at[land_down, target], g_down, to_s))
    halo_r = push(moves, dsend, drecv)

    for i in range(2):
        most = cells.at[i, pl.ds(0, planes * (n_sub - 1))]
        pltpu.make_async_copy(most, most, crecv.at[i]).wait()
        pltpu.make_async_copy(most, most, csend.at[i]).wait()
    for copy in fetches[2:]:
        copy.wait()
    spread_wait(0)

    def entry_of(row, i):
        return jnp.sum(jnp.where(lane == i, row, 0.0), axis=1, keepdims=True)

    def strain(q):
        after = lax.min(q + 1, n_grp - 1)
        row = sum(seen_at[q * n_sub + i] for i in range(n_sub))
        more = sum(seen_at[after * n_sub + i] for i in range(n_sub))
        more = jnp.where(q < n_grp - 1, more, 0.0)
        row = row + jnp.where(lane == 1, pltpu.roll(more, 125, 1), 0.0)
        values = [entry_of(row, i) for i in range(4)]
        return [v - values[0] for v in values[1:]]

    mine = sum(jnp.where(owners[q] == g, q, 0) for q in range(n_grp))
    mine = lax.min(mine, n_grp - 1)
    strength = sum(v * v for v in strain(mine))
    cond = cells[0] / (1.0 + cells[1] * strength)
    turned = [cond - K0]
    turned += [pltpu.roll(turned[0], i * side, 2) for i in range(1, per)]
    cube = (side, side, 128)
    cell_lane = lax.broadcasted_iota(jnp.int32, (1, 8, 128), 2)
    group = cell_lane // side
    in_group = lax.rem(cell_lane, side)
    parts = []
    for t in range(per):
        part = turned[(0 - t) % per]
        for j in range(1, per):
            part = jnp.where(group == j, turned[(j - t) % per], part)
        parts.append(part)
    shift_k = parts

    def ahead(v, axis):
        if axis == 0:
            return [jnp.concatenate([a[1:], a[:1]], 0) for a in v]
        if axis == 1:
            return v[1:] + [pltpu.roll(v[0], 7, 1)]
        return [
            jnp.where(in_group == side - 1, pltpu.roll(a, side - 1, 2), pltpu.roll(a, 127, 2))
            for a in v
        ]

    def behind(v, axis):
        if axis == 0:
            return [jnp.concatenate([a[-1:], a[:-1]], 0) for a in v]
        if axis == 1:
            return [pltpu.roll(v[-1], 1, 1)] + v[:-1]
        return [
            jnp.where(in_group == 0, pltpu.roll(a, 129 - side, 2), pltpu.roll(a, 1, 2)) for a in v
        ]

    def right(v):
        high, low = split(v)
        both = mm(jnp.concatenate([high, low], axis=1), turn_ref[...])
        return both[:, :128] + both[:, 128:]

    def left(t, v):
        high, low = split(v)
        both = mm(table_ref[t], high)
        return both[:wide] + both[wide:] + mm(table_ref[t, :wide], low)

    def halves(a, b, t):
        out = left(t, jnp.concatenate([a, b], axis=1))
        return out[:, :128], out[:, 128:]

    def along_z(v):
        return [right(a.reshape(wide, 128)).reshape(side, 8, 128) for a in v]

    def along_x(v):
        out = []
        for i in range(0, per, 2):
            for a in halves(v[i].reshape(wide, 128), v[i + 1].reshape(wide, 128), 1):
                out.append(a.reshape(side, 8, 128))
        return out

    def along_y(v):
        out = [[] for _ in range(per)]
        for i in range(0, side, 16):
            blocks = [
                jnp.concatenate([a[j : j + 8] for a in v], axis=1).reshape(wide, 128)
                for j in (i, i + 8)
            ]
            for block in halves(blocks[0], blocks[1], 0):
                block = block.reshape(8, side, 128)
                for t in range(per):
                    out[t].append(block[:, 8 * t : 8 * t + 8])
        return [jnp.concatenate(a, axis=0) for a in out]

    def solve(div):
        spectrum = along_x(along_y(along_z(div)))
        spectrum = [a * inverse_ref[:, 8 * t : 8 * t + 8] for t, a in enumerate(spectrum)]
        return along_z(along_y(along_x(spectrum)))

    def div_of(phi):
        out = [0.0] * per
        for axis in range(3):
            tau = [k * (a - b) for k, a, b in zip(shift_k, ahead(phi, axis), phi)]
            out = [o + a - b for o, a, b in zip(out, tau, behind(tau, axis))]
        return out

    backs = [behind(shift_k, axis) for axis in range(3)]
    div1 = []
    for t in range(per):
        back = jnp.where(group == 0, backs[0][t], shift_k[t])
        back = jnp.where(group == 1, backs[1][t], back)
        div1.append(shift_k[t] - jnp.where(group == 2, backs[2][t], back))
    phi1 = solve(div1)
    div2 = div_of(phi1)
    phi2 = solve(div2)
    div3 = div_of(phi2)
    first = [a + b for a, b in zip(div1, div2)]
    second = [a + b for a, b in zip(div2, div3)]
    volume = float(side**3)
    mean = total(cond) / volume
    entry = {}
    for turn in range(3):
        sums = 0.0
        for t in range(per):
            a = phi1[t] if turn == 0 else pltpu.roll(phi1[t], turn * side, 2)
            b = phi2[t] if turn == 0 else pltpu.roll(phi2[t], turn * side, 2)
            sums = sums + jnp.sum(a * first[t] + b * second[t], axis=0)
        sums = jnp.sum(sums, axis=0, keepdims=True)
        for j in range(turn, 3):
            value = -jnp.sum(
                jnp.where(lane // side == j, sums, 0.0), axis=1, keepdims=True
            ) / volume
            entry[j - turn, j] = entry[j, j - turn] = value + mean if turn == 0 else value
    row = jnp.zeros((1, 128), F32)
    for i in range(3):
        for j in range(3):
            row = row + jnp.where(lane == 3 * i + j, entry[i, j], 0.0)
    tan_ref[g] = row

    upper_g = (2 * g) // n_grp

    def tangent_send(k, carry):
        to_g = lax.rem(g + upper_g * k + (1 - upper_g) * (n_grp - k), n_grp)
        pltpu.make_async_remote_copy(
            src_ref=tan_ref.at[g], dst_ref=tan_ref.at[g], send_sem=tsend, recv_sem=trecv,
            device_id={"grp": to_g, "sub": s}, device_id_type=MESH,
        ).start()
        return carry

    lax.fori_loop(1, n_grp, tangent_send, 0, unroll=15)

    strains = [strain(p) for p in points]
    small = SHIFT * unit
    for i in range(win_x - 1):
        kz[i] = kz[i] * unit
    for copy in halo_r:
        copy.wait()

    most = tan_ref.at[pl.ds(0, n_grp - 1)]
    pltpu.make_async_copy(most, most, trecv).wait()
    pltpu.make_async_copy(most, most, tsend).wait()

    def tensor(p):
        row = tan_ref[owners[p]]
        return {(i, j): entry_of(row, 3 * i + j) for i in range(3) for j in range(i, 3)}

    tensors = [tensor(p) for p in points]

    def rows_times(t, d):
        return [
            sum(t[min(i, j), max(i, j)] * d[j] for j in range(3)) for i in range(3)
        ]

    def next_y(v):
        return jnp.where(y_at == win_y - 1, 0.0, pltpu.roll(v, win_y - 1, 0))

    def next_z(v):
        return jnp.where(z_at == rows_z - 1, 0.0, pltpu.roll(v, rows_z - 1, 1))

    def last_y(v):
        return jnp.where(y_at == 0, 0.0, pltpu.roll(v, 1, 0))

    def last_z(v):
        return jnp.where(z_at == 0, 0.0, pltpu.roll(v, 1, 1))

    def stencil(e):
        return last_y(e[1]) + last_z(e[2]) - e[0] - e[1] - e[2]

    fixes = []
    for t, d, mark in zip(tensors, strains, marks):
        e = [v * mark for v in rows_times(t, d)]
        fixes.append((e[0], stencil(e)))

    wide_at = [jnp.broadcast_to(x, plane) for x in spots]

    def fix(out, i, fixes, first):
        x, center = fixes[near(i)]
        out = out + jnp.where(wide_at[near(i)] == i, center, 0.0)
        if i > first:
            x, center = fixes[near(i - 1)]
            out = out + jnp.where(wide_at[near(i - 1)] == i - 1, x, 0.0)
        return out

    for i in range(win_x):
        value = win[i]
        if i < DEPTH:
            value = value * (g > 0).astype(F32)
        if i >= DEPTH + rows_x:
            value = value * (g < n_grp - 1).astype(F32)
        if within is not None:
            value = value * within
        out = fix(jnp.zeros(plane, F32), i, fixes, 0)
        if i == DEPTH + rows_x:
            out = out * (g < n_grp - 1).astype(F32)
        vs[0, i] = value - out

    unit_tensors = [
        {k: jnp.broadcast_to(v * unit, (8, 128)) for k, v in t.items()} for t in tensors
    ]

    sub_at = lax.broadcasted_iota(jnp.int32, (8, 128), 0)
    lane_at = lax.broadcasted_iota(jnp.int32, (8, 128), 1)
    tiles_y, tiles_z = win_y // 8, rows_z // 128
    cells_at = [(a, b) for a in range(tiles_y) for b in range(tiles_z)]

    def tiles_of(ref, *at):
        return {
            (a, b): ref[(*at, pl.ds(8 * a, 8), pl.ds(128 * b, 128))] for a, b in cells_at
        }

    def cut(v):
        return {(a, b): v[8 * a : 8 * a + 8, 128 * b : 128 * b + 128] for a, b in cells_at}

    def moved(v, axis, by):
        size = (8, 128)[axis]
        rolled = {key: pltpu.roll(w, by % size, axis) for key, w in v.items()}
        edge = (sub_at, lane_at)[axis] == (size - 1 if by < 0 else 0)
        out = {}
        for a, b in v:
            other = (a - by, b) if axis == 0 else (a, b - by)
            out[a, b] = jnp.where(edge, rolled.get(other, 0.0), rolled[a, b])
        return out

    spot_marks = [cut(mark) for mark in marks]
    spot_at = [jnp.broadcast_to(x, (8, 128)) for x in spots]
    hits = {(near(i), i): spot_at[near(i)] == i for i in range(win_x)}

    def advance(k):
        first, end = k, win_x - k
        node = NODES[k % BLOCK]
        keep = jnp.broadcast_to(small - node if node else small, (8, 128))
        v = tiles_of(vs, k, first)
        before = None
        for i in range(first, end - 1):
            after = tiles_of(vs, k, i + 1)
            weight = tiles_of(kz, i)
            n = near(i)
            up_y, up_z = moved(v, 0, -1), moved(v, 1, -1)
            q = [{}, {}, {}]
            for c in cells_at:
                mark = jnp.where(hits[n, i], spot_marks[n][c], 0.0)
                d = after[c] - v[c], up_y[c] - v[c], up_z[c] - v[c]
                extra = rows_times(unit_tensors[n], [mark * value for value in d])
                for j in range(3):
                    q[j][c] = weight[c] * d[j] + extra[j]
            if before is not None:
                low_y, low_z = moved(q[1], 0, 1), moved(q[2], 1, 1)
                for a, b in cells_at:
                    c = a, b
                    out = (before[c] - q[0][c]) + (low_y[c] - q[1][c])
                    out = out + ((low_z[c] - q[2][c]) + keep * v[c])
                    if i == DEPTH + rows_x:
                        out = out * (g < n_grp - 1).astype(F32)
                    if within is not None:
                        out = out * within[8 * a : 8 * a + 8, 128 * b : 128 * b + 128]
                    vs[k + 1, i, pl.ds(8 * a, 8), pl.ds(128 * b, 128)] = out
            before, v = q[0], after

    def own_of(k):
        return [vs[k, DEPTH + i, pl.ds(own_y, rows_y), :] for i in range(rows_x)]

    def dot(a, b):
        out = None
        for v, w in zip(a, b):
            out = add(out, v * w)
        parts = [
            out[i : i + 8, j : j + 128] for i in range(0, rows_y, 8) for j in range(0, rows_z, 128)
        ]
        return jnp.sum(sum(parts), axis=0, keepdims=True)

    def packed_row(parts, start=0):
        n = len(parts)
        column = jnp.sum(jnp.concatenate(parts, axis=0), axis=1, keepdims=True)
        down = lax.broadcasted_iota(jnp.int32, (n, 128), 0)
        across = lax.broadcasted_iota(jnp.int32, (n, 128), 1)
        return jnp.sum(jnp.where(across == down + start, column, 0.0), axis=0, keepdims=True)

    for k in range(BLOCK):
        advance(k)
    v = [own_of(k) for k in range(BLOCK + 1)]
    pairs = [(i, j) for i in range(BLOCK + 1) for j in range(i, BLOCK + 1)]
    spread_start(1, packed_row([dot(v[i], v[j]) for i, j in pairs]))
    for k in range(BLOCK, CG_ITERS):
        advance(k)
    for q in range(n_grp):
        chosen[q] = tan_ref[owners[q]]
    v += [own_of(k) for k in range(BLOCK + 1, CG_ITERS + 1)]

    has_point = (qy >= 0) & (qy < rows_y)
    here_x = lax.clamp(DEPTH, spots[1], DEPTH + rows_x - 1)
    here_y = lax.clamp(0, qy + own_y, win_y - 1)
    next_row = lax.clamp(0, qy + own_y + 1, win_y - 1)
    at_top = qy + own_y + 1 > win_y - 1
    here = (line == qz) & has_point
    slopes = []
    for k in range(CG_ITERS):
        base = vs[k, here_x, pl.ds(here_y, 1), :]
        side_x = vs[k, here_x + 1, pl.ds(here_y, 1), :]
        side_y = jnp.where(at_top, 0.0, vs[k, here_x, pl.ds(next_row, 1), :])
        side_z = jnp.where(line == rows_z - 1, 0.0, pltpu.roll(base, rows_z - 1, 1))
        for other in (side_x, side_y, side_z):
            value = jnp.where(here, other - base, 0.0)
            slopes.append(sum(value[:, j : j + 128] for j in range(0, rows_z, 128)))
    slope_at = 64
    slope_row = packed_row(slopes, slope_at)

    spread_wait(1)
    sums = jnp.sum(bc[0], axis=0)
    gram = {key: entry_of(sums, n) for n, key in enumerate(pairs)}
    one = [jnp.ones((1, 1), F32)]
    x_c, r_c, p_c = cg_steps(one, one, gram, times, False)
    r_powers, p_powers = raised(r_c, BLOCK - 1), raised(p_c, BLOCK)
    powers = r_powers + p_powers
    basis = [combine(c, v) for c in powers]
    width = BLOCK + BLOCK + 1
    pairs = [(i, j) for i in range(width) for j in range(i, width)]
    pairs = [key for key in pairs if key not in ((BLOCK - 1,) * 2, (BLOCK - 1, width - 1), (width - 1,) * 2)]
    spread_start(2, packed_row([dot(basis[i], basis[j]) for i, j in pairs]) + slope_row)
    x = combine(x_c, v)
    spot = lax.broadcasted_iota(jnp.int32, (n_grp, 1, 128), 2)
    rows_of = []
    for i in range(3):
        base = pltpu.roll(chosen[...], slope_at - 3 * i, 2)
        base = jnp.where((spot >= slope_at) & (spot < slope_at + 3), base, 0.0)
        rows_of.append(sum(pltpu.roll(base, 3 * k, 2) if k else base for k in range(CG_ITERS)))

    def image_of(c):
        c = c + [None] * (width - len(c))
        a, b = times(c[: BLOCK - 1]), times(c[BLOCK : width - 1])
        return a + [None] * (BLOCK - len(a)) + b

    spread_wait(2)
    got = bc[1]
    sums = jnp.sum(got, axis=0)
    gram = {key: entry_of(sums, n) for n, key in enumerate(pairs)}
    start = [None] * BLOCK + one
    x2_c, r2_c, _ = cg_steps(one, start, gram, image_of, True)
    x = combine([one[0]] + x2_c, [x] + basis)
    r = combine(r2_c, basis)
    for i in range(rows_x):
        field_ref[0, i] = x[i] * unit
        field_ref[1, i] = r[i]
    whole = x_c
    for c, power in zip(x2_c, powers):
        if c is not None:
            whole = plus(whole, scaled(power, c))
    slope = jnp.sum(got.reshape(n_grp, n_sub, 1, 128), axis=1)
    weights = jnp.zeros((1, 128), F32)
    for k in range(CG_ITERS):
        inside = (lane >= slope_at + 3 * k) & (lane < slope_at + 3 * k + 3)
        weights = weights + jnp.where(inside, whole[k] * unit, 0.0)
    slope = slope * weights[None]
    out = jnp.zeros_like(slope)
    for i in range(3):
        part = jnp.sum(slope * rows_of[i], axis=2, keepdims=True)
        out = out + jnp.where(spot == 9 + i, part, 0.0)
    for q in range(n_grp):
        small_ref[q : q + 1] = jnp.where(lane < 9, tan_ref[q], out[q])


def tables(side):
    index = np.arange(side)
    per = 128 // side
    place = np.arange(side).reshape(side // per, per).T.reshape(-1)
    angle = 2.0 * np.pi * (np.outer(index, index) % side) / side
    hartley = (np.cos(angle) + np.sin(angle)) / np.sqrt(side)

    def halves(a):
        a = a.astype(np.float32)
        high = a.astype(jnp.bfloat16)
        return high, (a - high.astype(np.float32)).astype(jnp.bfloat16)

    kinds = np.kron(np.eye(8), hartley[place][:, place]), np.kron(hartley, np.eye(8))
    table = np.stack([np.concatenate(halves(a), axis=0) for a in kinds])
    high, low = halves(np.kron(np.eye(per), hartley))
    turn = np.block([[high, low], [high, np.zeros_like(low)]])
    line = 4.0 * np.sin(np.pi * index / side) ** 2
    lam = line[:, None, None] + line[None, place, None] + line[None, None, :]
    lam[0, 0, 0] = 1.0
    inverse = 1.0 / (K0 * lam)
    inverse[0, 0, 0] = 0.0
    return table, turn, np.tile(inverse.astype(np.float32), (1, 1, per))


def body(displacement, load, kl_coef, damaged, owner, phase, soften):
    n_grp, n_sub = lax.axis_size("grp"), lax.axis_size("sub")
    count = n_grp * n_sub
    rows_x, rows_y, rows_z = displacement.shape
    planes = phase.shape[1]
    side = math.isqrt(phase.shape[2])
    table, turn, inverse = tables(side)
    points = owner.shape[0]
    win_x = rows_x + 2 * DEPTH
    win_y = rows_y + (EDGE if n_sub == 2 else 2 * EDGE)
    moves = 5 if n_sub == 2 else 8
    vmem = pl.BlockSpec(memory_space=pltpu.VMEM)
    smem = pl.BlockSpec(memory_space=pltpu.SMEM)
    fields, small = pl.pallas_call(
        functools.partial(kernel, n_grp, n_sub, side),
        out_shape=[
            jax.ShapeDtypeStruct((2, *displacement.shape), F32),
            jax.ShapeDtypeStruct((points, 128), F32),
        ],
        in_specs=[smem] * 3 + [pl.BlockSpec(memory_space=pl.ANY)] * 7,
        out_specs=[vmem] * 2,
        scratch_shapes=[
            pltpu.VMEM((n_grp, 1, 128), F32),
            pltpu.VMEM(displacement.shape, F32),
            pltpu.VMEM(displacement.shape, F32),
            pltpu.VMEM((win_x, win_y, rows_z), F32),
            pltpu.VMEM((win_x, win_y, rows_z), F32),
            pltpu.VMEM((CG_ITERS + 1, win_x, win_y, rows_z), F32),
            pltpu.VMEM((2, rows_x, 1, rows_z), F32),
            pltpu.VMEM((2, rows_y, rows_z), F32),
            pltpu.VMEM((2, rows_x, 1, rows_z), F32),
            pltpu.VMEM((2, side, side * side // 128, 128), F32),
            pltpu.VMEM((count, 1, 128), F32),
            pltpu.VMEM((2, count, 1, 128), F32),
            pltpu.VMEM((points, 1, 128), F32),
            pltpu.VMEM(table.shape, BF16),
            pltpu.VMEM(turn.shape, BF16),
            pltpu.VMEM(inverse.shape, F32),
            pltpu.SemaphoreType.DMA((4,)),
            pltpu.SemaphoreType.DMA((4,)),
            pltpu.SemaphoreType.DMA((moves,)),
            pltpu.SemaphoreType.DMA((moves,)),
            pltpu.SemaphoreType.DMA((2,)),
            pltpu.SemaphoreType.DMA((2,)),
            pltpu.SemaphoreType.DMA((3,)),
            pltpu.SemaphoreType.DMA((3,)),
            pltpu.SemaphoreType.DMA,
            pltpu.SemaphoreType.DMA,
            pltpu.SemaphoreType.DMA((5,)),
            pltpu.SemaphoreType.DMA((2,)),
        ],
        compiler_params=pltpu.CompilerParams(collective_id=0, has_side_effects=True),
    )(kl_coef, damaged, owner, displacement, load, phase, soften, jnp.asarray(table),
      jnp.asarray(turn), jnp.asarray(inverse))
    return fields[0], fields[1], small[:, :9], small[:, 9:12]


def solution(mesh):
    return jax.shard_map(
        body,
        mesh=mesh,
        in_specs=(
            P("grp", "sub", None), P("grp", "sub", None), P(), P(), P(),
            P("grp", "sub", None), P("grp", "sub", None),
        ),
        out_specs=(P("grp", "sub", None), P("grp", "sub", None), P(), P()),
        check_vma=False,
    )
```
